32 devices in a mesh: fold: 2 (over x), slab: 2 (over core), strip: 8 (over z, y).
Axes of the slice: x: 2, y: 2, z: 4, core: 2. Of those that a mesh axis runs over, the one named last changes fastest.
Arguments:
- volume: bfloat16 [128, 8, 128, 256], P('fold', 'slab', 'strip'), parts along dimension 0, may hold values from -6 to 6
- target: bfloat16 [512, 4, 64, 128], P('fold', 'slab', 'strip'), parts along dimension 0, may hold values from -6 to 6
- strided_weight: bfloat16 [128, 1728], replicated, may hold values from -0.15625 to 0.15625
- dilated_weight: bfloat16 [256, 3456], replicated, may hold values from -0.109375 to 0.109375
Outputs:
- prediction: bfloat16 [512, 4, 64, 128], P('fold', 'slab', 'strip'), parts along dimension 0
- strided_grad: float32 [256, 1728], P(('fold', 'strip')), parts along dimension 0
- dilated_grad: float32 [512, 3456], P(('fold', 'strip')), parts along dimension 0
The draws below stay inside these ranges and needn't reach their ends.
There are 2 independent parts, one for each index of `fold`. The reference program is written for one: setup_inputs(seed, part) draws one part's arguments, and reference() takes and returns one part's arrays. A program takes and returns all parts, laid end to end along the dimension named above; an argument that names none is the same for every part. Nothing has to cross between parts.
All inputs are finite; a program needn't handle non-finite values.
Results may differ from the reference program's by a relative error of at most 0.005.
Values may be sent and summed in bfloat16 or wider, within the bound.
No kernel may reach another device: no remote copies, remote signals or barrier semaphores. Data moves between devices by JAX's collectives and lax.ppermute only.
A program may use at most 128 MiB of HBM per device.

```python
import math
import jax
import jax.numpy as jnp
from jax import lax

C0 = 64
STRIDED_CHANNEL = 128
DILATED_CHANNEL = 256
DILATION_FACTOR = 2
NT = 256
NI = 8
NX = 128


def strengthened(result, key, source, target, shards_of, factor):
    def block_of(position):
        return (jnp.arange(result.shape[position]) // (result.shape[position] // shards_of)).reshape((-1,) + (1,) * (result.ndim - 1 - position))

    one_side = jax.random.permutation(key, shards_of)[block_of(target)]
    other_side = (block_of(target) + shards_of // 2) % shards_of
    return jnp.where((block_of(source) == one_side) | (block_of(source) == other_side), factor * result, result)


def block_levels(rng, shape, cuts, smallest, largest):
    factor_of = 1.0
    for dim, blocks in cuts:
        steps = jax.random.uniform(jax.random.fold_in(jax.random.fold_in(rng, 6), dim), (blocks,), jnp.float32, smallest / len(cuts), largest / len(cuts))
        factor_of = factor_of * jnp.repeat(jnp.exp(steps), shape[dim] // blocks).reshape((-1,) + (1,) * (len(shape) - 1 - dim))
    return factor_of


def centred(own_key, extent, width, reach, cuts=(), held_as=jnp.bfloat16):
    values = width * jax.random.normal(own_key, extent, jnp.float32)
    if cuts:
        values = values * block_levels(own_key, extent, cuts, -0.22, 0.18)
    return jnp.clip(values, -reach, reach).astype(held_as)


def gaussian_with(key, shape, deviation, limit, split, heavy, dtype=jnp.bfloat16):
    array = deviation * jax.random.normal(key, shape, jnp.float32)
    if split:
        array = array * block_levels(key, shape, split, -0.22, 0.18)
    return jnp.clip(strengthened(array, jax.random.fold_in(key, 3), *heavy), -limit, limit).astype(dtype)


def setup_inputs(seed: int = 0, part: int = 0) -> dict:
    seeds = jax.random.split(jax.random.key(seed), 5)
    own_keys = jax.random.split(jax.random.fold_in(seeds[4], part), 5)
    return {
        "volume": centred(own_keys[0], (C0, NI, NX, NT), 1.0, 6.0, ((1, 2), (2, 8))),
        "target": gaussian_with(own_keys[1], (DILATED_CHANNEL, NI // 2, NX // 2, NT // 2), 1.0, 6.0, ((1, 2), (2, 8)), (2, 0, 8, 2.0)),
        "strided_weight": centred(seeds[2], (STRIDED_CHANNEL, 27 * C0), (27 * C0) ** -0.5, 0.15625),
        "dilated_weight": centred(seeds[3], (DILATED_CHANNEL, 27 * STRIDED_CHANNEL), (27 * STRIDED_CHANNEL) ** -0.5, 0.109375),
    }


def silu_slope(value):
    sigma = jax.nn.sigmoid(value)
    return sigma * (1.0 + value * (1.0 - sigma))

def tap_list():
    return [(inline_stride, crossline_stride, time_stride) for inline_stride in range(3) for crossline_stride in range(3) for time_stride in range(3)]

def reference(volume, target, strided_weight, dilated_weight):
    row_halfspan = NI // 2
    column_halfspan = NX // 2
    depth_halfspan = NT // 2
    cell_count = row_halfspan * column_halfspan * depth_halfspan
    padded = jnp.pad(volume, ((0, 0), (1, 0), (1, 0), (1, 0)))

    def strided_window(inline_stride, crossline_stride, time_stride):
        kernel_window = lax.slice(padded, (0, inline_stride, crossline_stride, time_stride), (C0, inline_stride + 2 * row_halfspan - 1, crossline_stride + 2 * column_halfspan - 1, time_stride + 2 * depth_halfspan - 1), (1, 2, 2, 2))
        return kernel_window.reshape(C0, cell_count)

    def dilated_window(source_volume, channel_count, inline_stride, crossline_stride, time_stride):
        kernel_window = lax.slice(source_volume, (0, inline_stride * DILATION_FACTOR, crossline_stride * DILATION_FACTOR, time_stride * DILATION_FACTOR), (channel_count, inline_stride * DILATION_FACTOR + row_halfspan, crossline_stride * DILATION_FACTOR + column_halfspan, time_stride * DILATION_FACTOR + depth_halfspan))
        return kernel_window.reshape(channel_count, cell_count)
    taps = tap_list()
    preact = jnp.zeros((STRIDED_CHANNEL, cell_count), jnp.float32)
    for tap_index, (inline_stride, crossline_stride, time_stride) in enumerate(taps):
        block = strided_weight[:, tap_index * C0:(tap_index + 1) * C0]
        preact = preact + jnp.dot(block, strided_window(inline_stride, crossline_stride, time_stride), preferred_element_type=jnp.float32)
    hidden_state = jax.nn.silu(preact).astype(jnp.bfloat16)
    hidden_state_padded = jnp.pad(hidden_state.reshape(STRIDED_CHANNEL, row_halfspan, column_halfspan, depth_halfspan), ((0, 0), (DILATION_FACTOR, DILATION_FACTOR), (DILATION_FACTOR, DILATION_FACTOR), (DILATION_FACTOR, DILATION_FACTOR)))
    output = jnp.zeros((DILATED_CHANNEL, cell_count), jnp.float32)
    for tap_index, (inline_stride, crossline_stride, time_stride) in enumerate(taps):
        block = dilated_weight[:, tap_index * STRIDED_CHANNEL:(tap_index + 1) * STRIDED_CHANNEL]
        output = output + jnp.dot(block, dilated_window(hidden_state_padded, STRIDED_CHANNEL, inline_stride, crossline_stride, time_stride), preferred_element_type=jnp.float32)
    prediction = output.astype(jnp.bfloat16).reshape(DILATED_CHANNEL, row_halfspan, column_halfspan, depth_halfspan)
    residual_state = ((output - target.astype(jnp.float32).reshape(DILATED_CHANNEL, cell_count)) / math.sqrt(cell_count)).astype(jnp.bfloat16)
    dims = (((1,), (1,)), ((), ()))
    dilated_parts = []
    for inline_stride, crossline_stride, time_stride in taps:
        dilated_parts.append(lax.dot_general(residual_state, dilated_window(hidden_state_padded, STRIDED_CHANNEL, inline_stride, crossline_stride, time_stride), dims, preferred_element_type=jnp.float32))
    dilated_grad = jnp.concatenate(dilated_parts, axis=1)
    residual_state_padded = jnp.pad(residual_state.reshape(DILATED_CHANNEL, row_halfspan, column_halfspan, depth_halfspan), ((0, 0), (DILATION_FACTOR, DILATION_FACTOR), (DILATION_FACTOR, DILATION_FACTOR), (DILATION_FACTOR, DILATION_FACTOR)))
    hidden_grad = jnp.zeros((STRIDED_CHANNEL, cell_count), jnp.float32)
    for tap_index, (inline_stride, crossline_stride, time_stride) in enumerate(taps):
        block = dilated_weight[:, tap_index * STRIDED_CHANNEL:(tap_index + 1) * STRIDED_CHANNEL]
        kernel_window = dilated_window(residual_state_padded, DILATED_CHANNEL, 2 - inline_stride, 2 - crossline_stride, 2 - time_stride)
        hidden_grad = hidden_grad + lax.dot_general(block, kernel_window, (((0,), (0,)), ((), ())), preferred_element_type=jnp.float32)
    preact_grad = (hidden_grad * silu_slope(preact)).astype(jnp.bfloat16)
    strided_parts = []
    for inline_stride, crossline_stride, time_stride in taps:
        strided_parts.append(lax.dot_general(preact_grad, strided_window(inline_stride, crossline_stride, time_stride), dims, preferred_element_type=jnp.float32))
    strided_grad = jnp.concatenate(strided_parts, axis=1)
    return (prediction, strided_grad, dilated_grad)
```

```python
import math

import jax
import jax.numpy as jnp
from jax import lax
from jax.experimental import pallas as pl
from jax.experimental.pallas import tpu as pltpu
from jax.sharding import PartitionSpec as P


BF16 = jnp.bfloat16
F32 = jnp.float32
VMEM = pltpu.VMEM
VMEM_LIMIT = 24 * 1024 * 1024


def vmem_call(body, out_shape, n_in, scratch=()):
    spec = pl.BlockSpec(memory_space=pltpu.VMEM)
    return pl.pallas_call(
        body,
        out_shape=out_shape,
        in_specs=[spec] * n_in,
        out_specs=jax.tree.map(lambda _: spec, out_shape),
        scratch_shapes=list(scratch),
        compiler_params=pltpu.CompilerParams(vmem_limit_bytes=VMEM_LIMIT),
    )


def selection(depth):
    half = depth // 2
    source = lax.broadcasted_iota(jnp.int32, (depth, 3 * half), 0)
    lane = lax.broadcasted_iota(jnp.int32, (depth, 3 * half), 1)
    even = (lane < half) & (source == 2 * lane)
    odd = (lane >= half) & (lane < 2 * half) & (source == 2 * (lane - half) + 1)
    late = (lane >= 2 * half) & (source == 2 * (lane - 2 * half) - 1)
    return jnp.where(even | odd | late, 1.0, 0.0).astype(BF16)


def thirds(values):
    half = values.shape[1] // 3
    return [values[:, k * half : (k + 1) * half] for k in range(3)]


def spread(plane, pick, scratch):
    for k, part in enumerate(thirds(jnp.dot(plane, pick, preferred_element_type=F32))):
        scratch[k] = part


def put_column(vp_ref, values, channels, row, col, pairs):
    half = values[0].shape[1]
    taps = (values[2], values[0], values[1])
    for b in range(3):
        for h in range(2):
            rest = col + 1 - b - 2 * h
            if rest % 4 or not 0 <= rest // 4 < pairs:
                continue
            for c in range(3):
                start = ((row * 3 + b) * 3 + c) * channels
                vp_ref[rest // 4, start : start + channels, h * half : (h + 1) * half] = taps[c]


def split_body(vol_ref, tgt_ref, vp_ref, tp_ref, wide_ref, tall_ref):
    channels, rows, cols, depth = vol_ref.shape
    pairs = cols // 4
    half = depth // 2
    pick = selection(depth)
    for row in range(rows):
        slot = row % 2
        plane = vol_ref[:, row].reshape(channels * cols, depth)
        spread(plane, pick, wide_ref.at[slot])
        for col in range(cols):
            values = [
                wide_ref[slot, k, pl.ds(col, channels, stride=cols), :].astype(BF16)
                for k in range(3)
            ]
            put_column(vp_ref, values, channels, row + 1, col, pairs)
    outs, orows, ocols, _ = tgt_ref.shape
    for row in range(orows):
        slot = row % 2
        tall_ref[slot] = tgt_ref[:, row].astype(F32).reshape(outs * ocols, half)
        for col in range(ocols):
            values = tall_ref[slot, pl.ds(col, outs, stride=ocols), :].astype(BF16)
            tp_ref[row, col // 2, :, (col % 2) * half : (col % 2 + 1) * half] = values


def preact_body(own_ref, hrow_ref, hcol_ref, w_ref, vp_ref, h_ref, hl_ref, hr_ref, slope_ref, wide_ref):
    channels, cols, depth = hrow_ref.shape
    rows_ext = hcol_ref.shape[0]
    orows, pairs, _, _ = h_ref.shape
    vp_ref[:, 9 * channels :] = own_ref[:, 9 * channels :]
    pick = selection(depth)
    spread(hrow_ref[...].reshape(channels * cols, depth), pick, wide_ref)
    for col in range(cols):
        values = [
            wide_ref[k, pl.ds(col, channels, stride=cols), :].astype(BF16) for k in range(3)
        ]
        put_column(vp_ref, values, channels, 0, col, pairs)
    for row in range(rows_ext):
        values = jnp.dot(hcol_ref[row], pick, preferred_element_type=F32).astype(BF16)
        put_column(vp_ref, thirds(values), channels, row, -1, pairs)
    plane = 9 * channels
    for i in range(orows):
        for m in (0, pairs - 1, *range(1, pairs - 1)):
            window = vp_ref[m, 2 * i * plane : (2 * i + 3) * plane, :]
            pre = jnp.dot(w_ref[...], window, preferred_element_type=F32)
            sigma = jax.nn.sigmoid(pre)
            hidden = (pre * sigma).astype(BF16)
            h_ref[i, m] = hidden
            if m == 0:
                hl_ref[i] = hidden
            if m == pairs - 1:
                hr_ref[i] = hidden
            slope_ref[i, m] = sigma * (1.0 + pre * (1.0 - sigma))


def shifted(values, steps):
    half = values.shape[1] // 2
    lane = lax.broadcasted_iota(jnp.int32, (values.shape[0], half), 1)
    keep = lane >= steps if steps > 0 else lane < half + steps
    parts = [
        jnp.where(keep, pltpu.roll(values[:, k * half : (k + 1) * half], steps % half, 1), 0.0)
        for k in range(2)
    ]
    return jnp.concatenate(parts, axis=1)


def forward_body(
    scale, step, h_ref, hl_ref, hr_ref, o_ref, ol_ref, or_ref, w2_ref, wg_ref, tp_ref,
    hs_ref, pred_ref, res_ref, gown_ref, ghalo_ref, gother_ref, rs_ref,
):
    orows, pairs, mid, lanes = h_ref.shape
    outs = w2_ref.shape[0]
    for r in range(orows):
        for src, (whole, left, right) in enumerate(
            ((h_ref, hl_ref, hr_ref), (o_ref, ol_ref, or_ref))
        ):
            for x in range(pairs + 2):
                tile = left[r] if x == 0 else right[r] if x == pairs + 1 else whole[r, x - 1]
                wide = tile.astype(F32)
                base = src * 3 * mid
                hs_ref[r, x, base : base + mid, :] = shifted(wide, step).astype(BF16)
                hs_ref[r, x, base + mid : base + 2 * mid, :] = tile
                hs_ref[r, x, base + 2 * mid : base + 3 * mid, :] = shifted(wide, -step).astype(BF16)
    for r in range(orows):
        for m in range(pairs):
            window = hs_ref[r, m : m + 3].reshape(3 * 6 * mid, lanes)
            out = jnp.dot(w2_ref[...], window, preferred_element_type=F32)
            pred_ref[r, m] = out.astype(BF16)
            res = ((out - tp_ref[r, m].astype(F32)) * scale).astype(BF16)
            res_ref[r, m] = res
            wide = res.astype(F32)
            rs_ref[r, m, 0:outs, :] = shifted(wide, -step).astype(BF16)
            rs_ref[r, m, outs : 2 * outs, :] = res
            rs_ref[r, m, 2 * outs : 3 * outs, :] = shifted(wide, step).astype(BF16)
    block = 3 * outs
    for r in range(orows):
        for x in range(pairs + 2):
            low, high = max(x - 2, 0), min(x, pairs - 1)
            first = low - (x - 2)
            window = rs_ref[r, low : high + 1].reshape((high - low + 1) * block, lanes)
            weights = wg_ref[:, first * block : (first + high - low + 1) * block]
            grad = jnp.dot(weights, window, preferred_element_type=F32)
            gother_ref[r, x] = grad[mid:].astype(BF16)
            if x == 0:
                ghalo_ref[0, r] = grad[:mid]
            elif x == pairs + 1:
                ghalo_ref[1, r] = grad[:mid]
            else:
                gown_ref[r, x - 1] = grad[:mid]


NT = (((1,), (1,)), ((), ()))


def dilated_grad_body(res_ref, hs_ref, own_ref, other_ref):
    orows, pairs, outs, lanes = res_ref.shape
    mid = hs_ref.shape[2] // 6
    for b in range(3):
        for src, ref in enumerate((own_ref, other_ref)):
            base = src * 3 * mid
            total = None
            for r in range(orows):
                for m in range(pairs):
                    window = hs_ref[r, m + b, base : base + 3 * mid, :]
                    part = lax.dot_general(res_ref[r, m], window, NT, preferred_element_type=F32)
                    total = part if total is None else total + part
            ref[:, b * 3 * mid : (b + 1) * 3 * mid] = total


def strided_grad_body(gown_ref, gx_ref, gl_ref, gr_ref, slope_ref, vp_ref, out_ref):
    orows, pairs, mid, lanes = gown_ref.shape
    plane = vp_ref.shape[1] // (2 * orows + 1)
    total = None
    for i in range(orows):
        for m in range(pairs):
            grad = gown_ref[i, m] + gx_ref[i, m + 1].astype(F32)
            if m == 0:
                grad = grad + gl_ref[i].astype(F32)
            if m == pairs - 1:
                grad = grad + gr_ref[i].astype(F32)
            pg = (grad * slope_ref[i, m]).astype(BF16)
            window = vp_ref[m, 2 * i * plane : (2 * i + 3) * plane, :]
            part = lax.dot_general(pg, window, NT, preferred_element_type=F32)
            total = part if total is None else total + part
    out_ref[...] = total


def prediction_body(pred_ref, out_ref, tall_ref):
    orows, pairs, outs, lanes = pred_ref.shape
    half = lanes // 2
    cols = 2 * pairs
    for r in range(orows):
        slot = r % 2
        for col in range(cols):
            values = pred_ref[r, col // 2, :, (col % 2) * half : (col % 2 + 1) * half]
            tall_ref[slot, pl.ds(col, outs, stride=cols), :] = values.astype(F32)
        out_ref[:, r] = tall_ref[slot].reshape(outs, cols, half).astype(BF16)


def sds(shape, dtype):
    return jax.ShapeDtypeStruct(shape, dtype)


def shift_along(value, axis, steps):
    count = lax.axis_size(axis)
    pairs = [(i, i + steps) for i in range(count) if 0 <= i + steps < count]
    return lax.ppermute(value, axis, pairs)


def swap(value):
    return lax.ppermute(value, "slab", [(0, 1), (1, 0)])


def local(volume, target, strided_weight, dilated_weight):
    channels, rows_in, cols_in, depth = volume.shape
    mid = strided_weight.shape[0]
    outs = dilated_weight.shape[0]
    orows, ocols, half = rows_in // 2, cols_in // 2, depth // 2
    pairs, lanes = ocols // 2, 2 * half
    strips = lax.axis_size("strip")
    slab = lax.axis_index("slab")
    step = 2
    assert lax.axis_size("slab") == 2 and orows == step and ocols % 2 == 0
    cells = orows * ocols * half * lax.axis_size("slab") * strips
    scale = 1.0 / math.sqrt(cells)

    lower = shift_along(volume[:, -1], "slab", 1)
    last = jnp.concatenate([lower[None, :, -1, :], volume[:, :, -1, :].transpose(1, 0, 2)], axis=0)
    left = shift_along(last, "strip", 1)

    planes = dilated_weight.reshape(outs, 3, 9 * mid)
    w_own = planes[:, 1].reshape(outs, 3, 3 * mid)
    w_other = lax.dynamic_index_in_dim(planes, 2 - 2 * slab, 1, False).reshape(outs, 3, 3 * mid)
    both = jnp.stack([w_own, w_other], axis=2)
    w2 = both.reshape(outs, 18 * mid)
    wg = (
        both.reshape(outs, 3, 2, 3, mid)[:, ::-1]
        .transpose(2, 4, 1, 3, 0)
        .reshape(2 * mid, 9 * outs)
    )

    vp, tp = vmem_call(
        split_body,
        (
            sds((pairs, (rows_in + 1) * 9 * channels, lanes), BF16),
            sds((orows, pairs, outs, lanes), BF16),
        ),
        2,
        [VMEM((2, 3, channels * cols_in, half), F32), VMEM((2, outs * ocols, half), F32)],
    )(volume, target)
    vp, hidden, hid_l, hid_r, slope = vmem_call(
        preact_body,
        (
            sds(vp.shape, BF16),
            sds((orows, pairs, mid, lanes), BF16),
            sds((orows, mid, lanes), BF16),
            sds((orows, mid, lanes), BF16),
            sds((orows, pairs, mid, lanes), F32),
        ),
        4,
        [VMEM((3, channels * cols_in, half), F32)],
    )(vp, lower, left, strided_weight)

    from_left = shift_along(hid_r, "strip", 1)
    from_right = shift_along(hid_l, "strip", -1)
    other = swap(hidden)
    other_left = swap(from_left)
    other_right = swap(from_right)

    def forward(*refs):
        forward_body(scale, step, *refs)

    hs, pred, residual, gown, ghalo, gother = vmem_call(
        forward,
        (
            sds((orows, pairs + 2, 6 * mid, lanes), BF16),
            sds((orows, pairs, outs, lanes), BF16),
            sds((orows, pairs, outs, lanes), BF16),
            sds((orows, pairs, mid, lanes), F32),
            sds((2, orows, mid, lanes), F32),
            sds((orows, pairs + 2, mid, lanes), BF16),
        ),
        9,
        [VMEM((orows, pairs, 3 * outs, lanes), BF16)],
    )(hidden, from_left, from_right, other, other_left, other_right, w2, wg, tp)

    gx = swap(gother)
    to_left = (ghalo[0] + gx[:, 0].astype(F32)).astype(BF16)
    to_right = (ghalo[1] + gx[:, -1].astype(F32)).astype(BF16)
    grad_l = shift_along(to_right, "strip", 1)
    grad_r = shift_along(to_left, "strip", -1)

    dg_own, dg_other = vmem_call(
        dilated_grad_body, (sds((outs, 9 * mid), F32), sds((outs, 9 * mid), F32)), 2
    )(residual, hs)
    prediction = vmem_call(
        prediction_body,
        sds((outs, orows, ocols, half), BF16),
        1,
        [VMEM((2, outs * ocols, half), F32)],
    )(pred)
    sg = vmem_call(strided_grad_body, sds((mid, 27 * channels), F32), 6)(
        gown, gx, grad_l, grad_r, slope, vp
    )

    def halves(grad):
        rows = grad.shape[0] // strips
        return grad.reshape(strips, 2, rows // 2, grad.shape[1])

    def combined(grad):
        parts = halves(grad)
        mine = lax.dynamic_index_in_dim(parts, slab, 1, False)
        theirs = lax.dynamic_index_in_dim(parts, 1 - slab, 1, False)
        return mine + swap(theirs.astype(BF16)).astype(F32)

    rows = outs // strips
    dg = jnp.concatenate(
        [combined(dg_own).astype(BF16), dg_other.astype(BF16).reshape(strips, rows, 9 * mid)], axis=1
    )
    dg = lax.all_to_all(dg, "strip", 0, 0, tiled=True)
    dg = jnp.sum(dg.astype(F32), axis=0)
    sgc = lax.all_to_all(combined(sg).astype(BF16), "strip", 0, 0, tiled=True)
    sgc = jnp.sum(sgc.astype(F32), axis=0)
    dg_x, sg_x = swap(dg), swap(sgc)
    first = slab == 0
    half_rows = rows // 2
    dg0, dg1 = jnp.where(first, dg, dg_x), jnp.where(first, dg_x, dg)
    middle = jnp.concatenate([dg0[:half_rows], dg1[:half_rows]], axis=0)
    dilated_grad = jnp.concatenate([dg1[half_rows:], middle, dg0[half_rows:]], axis=1)
    strided_grad = jnp.concatenate(
        [jnp.where(first, sgc, sg_x), jnp.where(first, sg_x, sgc)], axis=0
    )
    return prediction, strided_grad, dilated_grad


def solution(mesh):
    return jax.shard_map(
        local,
        mesh=mesh,
        in_specs=(P("fold", "slab", "strip", None), P("fold", "slab", "strip", None), P(), P()),
        out_specs=(
            P("fold", "slab", "strip", None),
            P(("fold", "strip"), None),
            P(("fold", "strip"), None),
        ),
        check_vma=False,
    )
```

```python
import math

import jax
import jax.numpy as jnp
from jax import lax
from jax.experimental import pallas as pl
from jax.experimental.pallas import tpu as pltpu
from jax.sharding import PartitionSpec as P


BF16 = jnp.bfloat16
F32 = jnp.float32
VMEM = pltpu.VMEM
VMEM_LIMIT = 24 * 1024 * 1024


def vmem_call(body, out_shape, n_in, scratch=(), scalars=0):
    spec = pl.BlockSpec(memory_space=pltpu.VMEM)
    scalar = pl.BlockSpec(memory_space=pltpu.SMEM)
    return pl.pallas_call(
        body,
        out_shape=out_shape,
        in_specs=[scalar] * scalars + [spec] * n_in,
        out_specs=jax.tree.map(lambda _: spec, out_shape),
        scratch_shapes=list(scratch),
        compiler_params=pltpu.CompilerParams(vmem_limit_bytes=VMEM_LIMIT),
    )


def selection(depth):
    half = depth // 2
    source = lax.broadcasted_iota(jnp.int32, (depth, 3 * half), 0)
    lane = lax.broadcasted_iota(jnp.int32, (depth, 3 * half), 1)
    even = (lane < half) & (source == 2 * lane)
    odd = (lane >= half) & (lane < 2 * half) & (source == 2 * (lane - half) + 1)
    late = (lane >= 2 * half) & (source == 2 * (lane - 2 * half) - 1)
    return jnp.where(even | odd | late, 1.0, 0.0).astype(BF16)


def thirds(values):
    half = values.shape[1] // 3
    return [values[:, k * half : (k + 1) * half] for k in range(3)]


def spread(plane, pick, scratch):
    for k, part in enumerate(thirds(jnp.dot(plane, pick, preferred_element_type=F32))):
        scratch[k] = part


def put_column(vp_ref, values, channels, row, col, pairs):
    half = values[0].shape[1]
    taps = (values[2], values[0], values[1])
    for b in range(3):
        for h in range(2):
            rest = col + 1 - b - 2 * h
            if rest % 4 or not 0 <= rest // 4 < pairs:
                continue
            for c in range(3):
                start = ((row * 3 + b) * 3 + c) * channels
                vp_ref[rest // 4, start : start + channels, h * half : (h + 1) * half] = taps[c]


def split_body(vol_ref, tgt_ref, vp_ref, tp_ref, wide_ref, tall_ref):
    channels, rows, cols, depth = vol_ref.shape
    pairs = cols // 4
    half = depth // 2
    pick = selection(depth)
    for row in range(rows):
        slot = row % 2
        plane = vol_ref[:, row].reshape(channels * cols, depth)
        spread(plane, pick, wide_ref.at[slot])
        for col in range(cols):
            values = [
                wide_ref[slot, k, pl.ds(col, channels, stride=cols), :].astype(BF16)
                for k in range(3)
            ]
            put_column(vp_ref, values, channels, row + 1, col, pairs)
    outs, orows, ocols, _ = tgt_ref.shape
    for row in range(orows):
        slot = row % 2
        tall_ref[slot] = tgt_ref[:, row].astype(F32).reshape(outs * ocols, half)
        for col in range(ocols):
            values = tall_ref[slot, pl.ds(col, outs, stride=ocols), :].astype(BF16)
            tp_ref[row, col // 2, :, (col % 2) * half : (col % 2 + 1) * half] = values


def preact_body(own_ref, hrow_ref, hcol_ref, w_ref, vp_ref, h_ref, hl_ref, hr_ref, slope_ref, wide_ref):
    channels, cols, depth = hrow_ref.shape
    rows_ext = hcol_ref.shape[0]
    orows, pairs, _, _ = h_ref.shape
    vp_ref[:, 9 * channels :] = own_ref[:, 9 * channels :]
    pick = selection(depth)
    spread(hrow_ref[...].reshape(channels * cols, depth), pick, wide_ref)
    for col in range(cols):
        values = [
            wide_ref[k, pl.ds(col, channels, stride=cols), :].astype(BF16) for k in range(3)
        ]
        put_column(vp_ref, values, channels, 0, col, pairs)
    for row in range(rows_ext):
        values = jnp.dot(hcol_ref[row], pick, preferred_element_type=F32).astype(BF16)
        put_column(vp_ref, thirds(values), channels, row, -1, pairs)
    plane = 9 * channels
    for i in range(orows):
        for m in (0, pairs - 1, *range(1, pairs - 1)):
            window = vp_ref[m, 2 * i * plane : (2 * i + 3) * plane, :]
            pre = jnp.dot(w_ref[...], window, preferred_element_type=F32)
            sigma = jax.nn.sigmoid(pre)
            hidden = (pre * sigma).astype(BF16)
            h_ref[i, m] = hidden
            if m == 0:
                hl_ref[i] = hidden
            if m == pairs - 1:
                hr_ref[i] = hidden
            slope_ref[i, m] = sigma * (1.0 + pre * (1.0 - sigma))


def shifted(values, steps):
    half = values.shape[1] // 2
    lane = lax.broadcasted_iota(jnp.int32, (values.shape[0], half), 1)
    keep = lane >= steps if steps > 0 else lane < half + steps
    parts = [
        jnp.where(keep, pltpu.roll(values[:, k * half : (k + 1) * half], steps % half, 1), 0.0)
        for k in range(2)
    ]
    return jnp.concatenate(parts, axis=1)


def weights_body(slab_ref, wd_ref, ws_ref, w2_ref, wg_ref, wst_ref):
    outs, width = wd_ref.shape
    mid = width // 27
    wst_ref[...] = ws_ref[...].T

    def fill(src, a):
        for b in range(3):
            block = (a * 3 + b) * 3 * mid
            to = (b * 2 + src) * 3 * mid
            w2_ref[:, to : to + 3 * mid] = wd_ref[:, block : block + 3 * mid]
            for c in range(3):
                tap = wd_ref[:, block + c * mid : block + (c + 1) * mid]
                column = ((2 - b) * 3 + c) * outs
                wg_ref[src * mid : (src + 1) * mid, column : column + outs] = tap.T

    fill(0, 1)

    @pl.when(slab_ref[0] == 0)
    def _():
        fill(1, 2)

    @pl.when(slab_ref[0] != 0)
    def _():
        fill(1, 0)


def forward_body(
    scale, step, h_ref, hl_ref, hr_ref, o_ref, ol_ref, or_ref, w2_ref, tp_ref,
    hs_ref, pred_ref, rs_ref,
):
    orows, pairs, mid, lanes = h_ref.shape
    outs = w2_ref.shape[0]
    for r in range(orows):
        for src, (whole, left, right) in enumerate(
            ((h_ref, hl_ref, hr_ref), (o_ref, ol_ref, or_ref))
        ):
            for x in range(pairs + 2):
                tile = left[r] if x == 0 else right[r] if x == pairs + 1 else whole[r, x - 1]
                wide = tile.astype(F32)
                base = src * 3 * mid
                hs_ref[r, x, base : base + mid, :] = shifted(wide, step).astype(BF16)
                hs_ref[r, x, base + mid : base + 2 * mid, :] = tile
                hs_ref[r, x, base + 2 * mid : base + 3 * mid, :] = shifted(wide, -step).astype(BF16)
    for r in range(orows):
        for m in range(pairs):
            window = hs_ref[r, m : m + 3].reshape(3 * 6 * mid, lanes)
            out = jnp.dot(w2_ref[...], window, preferred_element_type=F32)
            pred_ref[r, m] = out.astype(BF16)
            res = ((out - tp_ref[r, m].astype(F32)) * scale).astype(BF16)
            wide = res.astype(F32)
            rs_ref[r, m, 0:outs, :] = shifted(wide, -step).astype(BF16)
            rs_ref[r, m, outs : 2 * outs, :] = res
            rs_ref[r, m, 2 * outs : 3 * outs, :] = shifted(wide, step).astype(BF16)


def hidden_grad_body(rs_ref, wg_ref, gown_ref, ghalo_ref, gother_ref):
    orows, pairs, block, lanes = rs_ref.shape
    mid = gown_ref.shape[2]
    for r in range(orows):
        for x in range(pairs + 2):
            low, high = max(x - 2, 0), min(x, pairs - 1)
            first = low - (x - 2)
            window = rs_ref[r, low : high + 1].reshape((high - low + 1) * block, lanes)
            weights = wg_ref[:, first * block : (first + high - low + 1) * block]
            grad = jnp.dot(weights, window, preferred_element_type=F32)
            gother_ref[r, x] = grad[mid:].astype(BF16)
            if x == 0:
                ghalo_ref[0, r] = grad[:mid]
            elif x == pairs + 1:
                ghalo_ref[1, r] = grad[:mid]
            else:
                gown_ref[r, x - 1] = grad[:mid]


NT = (((1,), (1,)), ((), ()))


def split_rows(slab_ref, total, mine_ref, send_ref, columns):
    strips, rows, _ = mine_ref.shape
    parts = total.reshape(strips, 2, rows, total.shape[1])
    first = slab_ref[0] == 0
    mine_ref[:, :, columns] = jnp.where(first, parts[:, 0], parts[:, 1])
    send_ref[:, :, columns] = jnp.where(first, parts[:, 1], parts[:, 0]).astype(BF16)


def dilated_grad_body(slab_ref, rs_ref, hs_ref, mine_ref, send_ref, other_ref):
    orows, pairs, block, lanes = rs_ref.shape
    outs = block // 3
    mid = hs_ref.shape[2] // 6
    for b in range(3):
        columns = slice(b * 3 * mid, (b + 1) * 3 * mid)
        for src in range(2):
            base = src * 3 * mid
            total = None
            for r in range(orows):
                for m in range(pairs):
                    window = hs_ref[r, m + b, base : base + 3 * mid, :]
                    part = lax.dot_general(
                        rs_ref[r, m, outs : 2 * outs, :], window, NT, preferred_element_type=F32
                    )
                    total = part if total is None else total + part
            if src == 0:
                split_rows(slab_ref, total, mine_ref, send_ref, columns)
            else:
                strips, rows, _ = other_ref.shape
                other_ref[:, :, columns] = total.reshape(strips, rows, 3 * mid).astype(BF16)


def strided_grad_body(slab_ref, gown_ref, gx_ref, gl_ref, gr_ref, slope_ref, vp_ref, mine_ref, send_ref):
    orows, pairs, mid, lanes = gown_ref.shape
    plane = vp_ref.shape[1] // (2 * orows + 1)
    total = None
    for i in range(orows):
        for m in range(pairs):
            grad = gown_ref[i, m] + gx_ref[i, m + 1].astype(F32)
            if m == 0:
                grad = grad + gl_ref[i].astype(F32)
            if m == pairs - 1:
                grad = grad + gr_ref[i].astype(F32)
            pg = (grad * slope_ref[i, m]).astype(BF16)
            window = vp_ref[m, 2 * i * plane : (2 * i + 3) * plane, :]
            part = lax.dot_general(pg, window, NT, preferred_element_type=F32)
            total = part if total is None else total + part
    split_rows(slab_ref, total, mine_ref, send_ref, slice(None))


def prediction_body(pred_ref, out_ref, tall_ref):
    orows, pairs, outs, lanes = pred_ref.shape
    half = lanes // 2
    cols = 2 * pairs
    for r in range(orows):
        slot = r % 2
        for col in range(cols):
            values = pred_ref[r, col // 2, :, (col % 2) * half : (col % 2 + 1) * half]
            tall_ref[slot, pl.ds(col, outs, stride=cols), :] = values.astype(F32)
        out_ref[:, r] = tall_ref[slot].reshape(outs, cols, half).astype(BF16)


def sds(shape, dtype):
    return jax.ShapeDtypeStruct(shape, dtype)


def shift_along(value, axis, steps):
    count = lax.axis_size(axis)
    pairs = [(i, i + steps) for i in range(count) if 0 <= i + steps < count]
    return lax.ppermute(value, axis, pairs)


def swap(value):
    return lax.ppermute(value, "slab", [(0, 1), (1, 0)])


def local(volume, target, strided_weight, dilated_weight):
    channels, rows_in, cols_in, depth = volume.shape
    mid = strided_weight.shape[0]
    outs = dilated_weight.shape[0]
    orows, ocols, half = rows_in // 2, cols_in // 2, depth // 2
    pairs, lanes = ocols // 2, 2 * half
    strips = lax.axis_size("strip")
    slab = lax.axis_index("slab")
    slab_id = slab.reshape(1).astype(jnp.int32)
    step = 2
    assert lax.axis_size("slab") == 2 and orows == step and ocols % 2 == 0
    cells = orows * ocols * half * lax.axis_size("slab") * strips
    scale = 1.0 / math.sqrt(cells)

    lower = shift_along(volume[:, -1], "slab", 1)
    last = jnp.concatenate([lower[None, :, -1, :], volume[:, :, -1, :].transpose(1, 0, 2)], axis=0)
    left = shift_along(last, "strip", 1)

    w2, wg, ws = vmem_call(
        weights_body,
        (
            sds((outs, 18 * mid), BF16),
            sds((2 * mid, 9 * outs), BF16),
            sds((mid, 27 * channels), BF16),
        ),
        2,
        scalars=1,
    )(slab_id, dilated_weight, strided_weight.T)
    vp, tp = vmem_call(
        split_body,
        (
            sds((pairs, (rows_in + 1) * 9 * channels, lanes), BF16),
            sds((orows, pairs, outs, lanes), BF16),
        ),
        2,
        [VMEM((2, 3, channels * cols_in, half), F32), VMEM((2, outs * ocols, half), F32)],
    )(volume, target)
    vp, hidden, hid_l, hid_r, slope = vmem_call(
        preact_body,
        (
            sds(vp.shape, BF16),
            sds((orows, pairs, mid, lanes), BF16),
            sds((orows, mid, lanes), BF16),
            sds((orows, mid, lanes), BF16),
            sds((orows, pairs, mid, lanes), F32),
        ),
        4,
        [VMEM((3, channels * cols_in, half), F32)],
    )(vp, lower, left, ws)

    from_left = shift_along(hid_r, "strip", 1)
    from_right = shift_along(hid_l, "strip", -1)
    other = swap(hidden)
    other_left = swap(from_left)
    other_right = swap(from_right)

    def forward(*refs):
        forward_body(scale, step, *refs)

    hs, pred, residual = vmem_call(
        forward,
        (
            sds((orows, pairs + 2, 6 * mid, lanes), BF16),
            sds((orows, pairs, outs, lanes), BF16),
            sds((orows, pairs, 3 * outs, lanes), BF16),
        ),
        8,
    )(hidden, from_left, from_right, other, other_left, other_right, w2, tp)

    rows = outs // strips
    half_rows = rows // 2
    mine, send, apart = vmem_call(
        dilated_grad_body,
        (
            sds((strips, half_rows, 9 * mid), F32),
            sds((strips, half_rows, 9 * mid), BF16),
            sds((strips, rows, 9 * mid), BF16),
        ),
        2,
        scalars=1,
    )(slab_id, residual, hs)
    dg = jnp.concatenate([(mine + swap(send).astype(F32)).astype(BF16), apart], axis=1)
    dg, residual = lax.optimization_barrier((dg, residual))
    dg = lax.all_to_all(dg, "strip", 0, 0, tiled=True)

    gown, ghalo, gother = vmem_call(
        hidden_grad_body,
        (
            sds((orows, pairs, mid, lanes), F32),
            sds((2, orows, mid, lanes), F32),
            sds((orows, pairs + 2, mid, lanes), BF16),
        ),
        2,
    )(residual, wg)

    gx = swap(gother)
    to_left = (ghalo[0] + gx[:, 0].astype(F32)).astype(BF16)
    to_right = (ghalo[1] + gx[:, -1].astype(F32)).astype(BF16)
    grad_l = shift_along(to_right, "strip", 1)
    grad_r = shift_along(to_left, "strip", -1)

    prediction = vmem_call(
        prediction_body,
        sds((outs, orows, ocols, half), BF16),
        1,
        [VMEM((2, outs * ocols, half), F32)],
    )(pred)
    mid_rows = mid // strips // 2
    smine, ssend = vmem_call(
        strided_grad_body,
        (
            sds((strips, mid_rows, 27 * channels), F32),
            sds((strips, mid_rows, 27 * channels), BF16),
        ),
        6,
        scalars=1,
    )(slab_id, gown, gx, grad_l, grad_r, slope, vp)
    sg = (smine + swap(ssend).astype(F32)).astype(BF16)
    sg = lax.all_to_all(sg, "strip", 0, 0, tiled=True)

    sg = jnp.sum(sg.astype(F32), axis=0)
    dg = jnp.sum(dg.astype(F32), axis=0)
    dg_x, sg_x = swap(dg), swap(sg)
    first = slab == 0
    dg0, dg1 = jnp.where(first, dg, dg_x), jnp.where(first, dg_x, dg)
    middle = jnp.concatenate([dg0[:half_rows], dg1[:half_rows]], axis=0)
    dilated_grad = jnp.concatenate([dg1[half_rows:], middle, dg0[half_rows:]], axis=1)
    strided_grad = jnp.concatenate(
        [jnp.where(first, sg, sg_x), jnp.where(first, sg_x, sg)], axis=0
    )
    return prediction, strided_grad, dilated_grad


def solution(mesh):
    return jax.shard_map(
        local,
        mesh=mesh,
        in_specs=(P("fold", "slab", "strip", None), P("fold", "slab", "strip", None), P(), P()),
        out_specs=(
            P("fold", "slab", "strip", None),
            P(("fold", "strip"), None),
            P(("fold", "strip"), None),
        ),
        check_vma=False,
    )
```

```python
import math

import jax
import jax.numpy as jnp
from jax import lax
from jax.experimental import pallas as pl
from jax.experimental.pallas import tpu as pltpu
from jax.sharding import PartitionSpec as P


BF16 = jnp.bfloat16
F32 = jnp.float32
VMEM = pltpu.VMEM
VMEM_LIMIT = 20 * 1024 * 1024


def vmem_call(body, out_shape, n_in, scratch=(), scalars=0):
    spec = pl.BlockSpec(memory_space=pltpu.VMEM)
    scalar = pl.BlockSpec(memory_space=pltpu.SMEM)
    return pl.pallas_call(
        body,
        out_shape=out_shape,
        in_specs=[scalar] * scalars + [spec] * n_in,
        out_specs=jax.tree.map(lambda _: spec, out_shape),
        scratch_shapes=list(scratch),
        compiler_params=pltpu.CompilerParams(vmem_limit_bytes=VMEM_LIMIT),
    )


def selection(depth):
    half = depth // 2
    source = lax.broadcasted_iota(jnp.int32, (depth, 3 * half), 0)
    lane = lax.broadcasted_iota(jnp.int32, (depth, 3 * half), 1)
    even = (lane < half) & (source == 2 * lane)
    odd = (lane >= half) & (lane < 2 * half) & (source == 2 * (lane - half) + 1)
    late = (lane >= 2 * half) & (source == 2 * (lane - 2 * half) - 1)
    return jnp.where(even | odd | late, 1.0, 0.0).astype(BF16)


def thirds(values):
    half = values.shape[1] // 3
    return [values[:, k * half : (k + 1) * half] for k in range(3)]


def spread(plane, pick, scratch):
    for k, part in enumerate(thirds(jnp.dot(plane, pick, preferred_element_type=F32))):
        scratch[k] = part


def put_column(vp_ref, values, channels, row, col, pairs):
    half = values[0].shape[1]
    taps = (values[2], values[0], values[1])
    for b in range(3):
        for h in range(2):
            rest = col + 1 - b - 2 * h
            if rest % 4 or not 0 <= rest // 4 < pairs:
                continue
            for c in range(3):
                start = ((row * 3 + b) * 3 + c) * channels
                vp_ref[rest // 4, start : start + channels, h * half : (h + 1) * half] = taps[c]


def split_body(vol_ref, tgt_ref, vp_ref, tp_ref, wide_ref, tall_ref):
    channels, rows, cols, depth = vol_ref.shape
    pairs = cols // 4
    half = depth // 2
    pick = selection(depth)
    for row in range(rows):
        slot = row % 2
        plane = vol_ref[:, row].reshape(channels * cols, depth)
        spread(plane, pick, wide_ref.at[slot])
        for col in range(cols):
            values = [
                wide_ref[slot, k, pl.ds(col, channels, stride=cols), :].astype(BF16)
                for k in range(3)
            ]
            put_column(vp_ref, values, channels, row + 1, col, pairs)
    outs, orows, ocols, _ = tgt_ref.shape
    for row in range(orows):
        slot = row % 2
        tall_ref[slot] = tgt_ref[:, row].astype(F32).reshape(outs * ocols, half)
        for col in range(ocols):
            values = tall_ref[slot, pl.ds(col, outs, stride=ocols), :].astype(BF16)
            tp_ref[row, col // 2, :, (col % 2) * half : (col % 2 + 1) * half] = values


def preact_body(own_ref, hrow_ref, hcol_ref, w_ref, vp_ref, h_ref, hl_ref, hr_ref, slope_ref, wide_ref):
    channels, cols, depth = hrow_ref.shape
    rows_ext = hcol_ref.shape[0]
    orows, pairs, _, _ = h_ref.shape
    vp_ref[:, 9 * channels :] = own_ref[:, 9 * channels :]
    pick = selection(depth)
    spread(hrow_ref[...].reshape(channels * cols, depth), pick, wide_ref)
    for col in range(cols):
        values = [
            wide_ref[k, pl.ds(col, channels, stride=cols), :].astype(BF16) for k in range(3)
        ]
        put_column(vp_ref, values, channels, 0, col, pairs)
    for row in range(rows_ext):
        values = jnp.dot(hcol_ref[row], pick, preferred_element_type=F32).astype(BF16)
        put_column(vp_ref, thirds(values), channels, row, -1, pairs)
    plane = 9 * channels
    for i in range(orows):
        for m in (0, pairs - 1, *range(1, pairs - 1)):
            window = vp_ref[m, 2 * i * plane : (2 * i + 3) * plane, :]
            pre = jnp.dot(w_ref[...], window, preferred_element_type=F32)
            sigma = jax.nn.sigmoid(pre)
            hidden = (pre * sigma).astype(BF16)
            h_ref[i, m] = hidden
            if m == 0:
                hl_ref[i] = hidden
            if m == pairs - 1:
                hr_ref[i] = hidden
            slope_ref[i, m] = sigma * (1.0 + pre * (1.0 - sigma))


def shifted(values, steps):
    half = values.shape[1] // 2
    lane = lax.broadcasted_iota(jnp.int32, (values.shape[0], half), 1)
    keep = lane >= steps if steps > 0 else lane < half + steps
    parts = [
        jnp.where(keep, pltpu.roll(values[:, k * half : (k + 1) * half], steps % half, 1), 0.0)
        for k in range(2)
    ]
    return jnp.concatenate(parts, axis=1)


def weights_body(slab_ref, wd_ref, ws_ref, w2_ref, wg_ref, wst_ref):
    outs, width = wd_ref.shape
    mid = width // 27
    wst_ref[...] = ws_ref[...].T

    def fill(src, a):
        for b in range(3):
            block = (a * 3 + b) * 3 * mid
            to = (b * 2 + src) * 3 * mid
            w2_ref[:, to : to + 3 * mid] = wd_ref[:, block : block + 3 * mid]
            for c in range(3):
                tap = wd_ref[:, block + c * mid : block + (c + 1) * mid]
                column = ((2 - b) * 3 + c) * outs
                wg_ref[src * mid : (src + 1) * mid, column : column + outs] = tap.T

    fill(0, 1)

    @pl.when(slab_ref[0] == 0)
    def _():
        fill(1, 2)

    @pl.when(slab_ref[0] != 0)
    def _():
        fill(1, 0)


def forward_body(
    scale, step, h_ref, hl_ref, hr_ref, o_ref, ol_ref, or_ref, w2_ref, tp_ref,
    hs_ref, pred_ref, rs_ref,
):
    orows, pairs, mid, lanes = h_ref.shape
    outs = w2_ref.shape[0]
    for r in range(orows):
        for src, (whole, left, right) in enumerate(
            ((h_ref, hl_ref, hr_ref), (o_ref, ol_ref, or_ref))
        ):
            for x in range(pairs + 2):
                tile = left[r] if x == 0 else right[r] if x == pairs + 1 else whole[r, x - 1]
                wide = tile.astype(F32)
                base = src * 3 * mid
                hs_ref[r, x, base : base + mid, :] = shifted(wide, step).astype(BF16)
                hs_ref[r, x, base + mid : base + 2 * mid, :] = tile
                hs_ref[r, x, base + 2 * mid : base + 3 * mid, :] = shifted(wide, -step).astype(BF16)
    for r in range(orows):
        for m in range(pairs):
            window = hs_ref[r, m : m + 3].reshape(3 * 6 * mid, lanes)
            out = jnp.dot(w2_ref[...], window, preferred_element_type=F32)
            pred_ref[r, m] = out.astype(BF16)
            res = ((out - tp_ref[r, m].astype(F32)) * scale).astype(BF16)
            wide = res.astype(F32)
            rs_ref[r, m, 0:outs, :] = shifted(wide, -step).astype(BF16)
            rs_ref[r, m, outs : 2 * outs, :] = res
            rs_ref[r, m, 2 * outs : 3 * outs, :] = shifted(wide, step).astype(BF16)


def hidden_grad_body(rs_ref, wg_ref, gown_ref, ghalo_ref, gother_ref):
    orows, pairs, block, lanes = rs_ref.shape
    mid = gown_ref.shape[2]
    for r in range(orows):
        for x in range(pairs + 2):
            low, high = max(x - 2, 0), min(x, pairs - 1)
            first = low - (x - 2)
            window = rs_ref[r, low : high + 1].reshape((high - low + 1) * block, lanes)
            weights = wg_ref[:, first * block : (first + high - low + 1) * block]
            grad = jnp.dot(weights, window, preferred_element_type=F32)
            gother_ref[x, r] = grad[mid:].astype(BF16)
            if x == 0:
                ghalo_ref[0, r] = grad[:mid]
            elif x == pairs + 1:
                ghalo_ref[1, r] = grad[:mid]
            else:
                gown_ref[r, x - 1] = grad[:mid]


NT = (((1,), (1,)), ((), ()))


def split_rows(slab_ref, total, mine_ref, send_ref, columns):
    strips, rows, _ = mine_ref.shape
    parts = total.reshape(strips, 2, rows, total.shape[1])
    first = slab_ref[0] == 0
    mine_ref[:, :, columns] = jnp.where(first, parts[:, 0], parts[:, 1])
    send_ref[:, :, columns] = jnp.where(first, parts[:, 1], parts[:, 0]).astype(BF16)


def dilated_grad_body(slab_ref, rs_ref, hs_ref, mine_ref, send_ref, other_ref):
    orows, pairs, block, lanes = rs_ref.shape
    outs = block // 3
    mid = hs_ref.shape[2] // 6
    for b in range(3):
        columns = slice(b * 3 * mid, (b + 1) * 3 * mid)
        for src in range(2):
            base = src * 3 * mid
            total = None
            for r in range(orows):
                for m in range(pairs):
                    window = hs_ref[r, m + b, base : base + 3 * mid, :]
                    part = lax.dot_general(
                        rs_ref[r, m, outs : 2 * outs, :], window, NT, preferred_element_type=F32
                    )
                    total = part if total is None else total + part
            if src == 0:
                split_rows(slab_ref, total, mine_ref, send_ref, columns)
            else:
                strips, rows, _ = other_ref.shape
                other_ref[:, :, columns] = total.reshape(strips, rows, 3 * mid).astype(BF16)


def strided_grad_body(slab_ref, gown_ref, gx_ref, gl_ref, gr_ref, slope_ref, vp_ref, mine_ref, send_ref):
    orows, pairs, mid, lanes = gown_ref.shape
    plane = vp_ref.shape[1] // (2 * orows + 1)
    total = None
    for i in range(orows):
        for m in range(pairs):
            grad = gown_ref[i, m] + gx_ref[m + 1, i].astype(F32)
            if m == 0:
                grad = grad + gl_ref[i].astype(F32)
            if m == pairs - 1:
                grad = grad + gr_ref[i].astype(F32)
            pg = (grad * slope_ref[i, m]).astype(BF16)
            window = vp_ref[m, 2 * i * plane : (2 * i + 3) * plane, :]
            part = lax.dot_general(pg, window, NT, preferred_element_type=F32)
            total = part if total is None else total + part
    width = mine_ref.shape[2]
    pad = jnp.zeros((mid, 2 * width - total.shape[1]), F32)
    low, high = total[:, :width], jnp.concatenate([total[:, width:], pad], axis=1)
    first = slab_ref[0] == 0
    mine_ref[...] = jnp.where(first, low, high).reshape(mine_ref.shape)
    send_ref[...] = jnp.where(first, high, low).reshape(mine_ref.shape).astype(BF16)


def prediction_body(pred_ref, out_ref, tall_ref):
    orows, pairs, outs, lanes = pred_ref.shape
    half = lanes // 2
    cols = 2 * pairs
    for r in range(orows):
        slot = r % 2
        for col in range(cols):
            values = pred_ref[r, col // 2, :, (col % 2) * half : (col % 2 + 1) * half]
            tall_ref[slot, pl.ds(col, outs, stride=cols), :] = values.astype(F32)
        out_ref[:, r] = tall_ref[slot].reshape(outs, cols, half).astype(BF16)


def sds(shape, dtype):
    return jax.ShapeDtypeStruct(shape, dtype)


def shift_along(value, axis, steps):
    count = lax.axis_size(axis)
    pairs = [(i, i + steps) for i in range(count) if 0 <= i + steps < count]
    return lax.ppermute(value, axis, pairs)


def swap(value):
    return lax.ppermute(value, "slab", [(0, 1), (1, 0)])


def local(volume, target, strided_weight, dilated_weight):
    channels, rows_in, cols_in, depth = volume.shape
    mid = strided_weight.shape[0]
    outs = dilated_weight.shape[0]
    orows, ocols, half = rows_in // 2, cols_in // 2, depth // 2
    pairs, lanes = ocols // 2, 2 * half
    strips = lax.axis_size("strip")
    slab = lax.axis_index("slab")
    strip = lax.axis_index("strip")
    groups = strips // 2
    place, parity = strip // 2, strip % 2
    scalars = (slab == 0, slab, parity, 1 - parity, *((place + d) % groups for d in range(groups)))
    target, scalars = lax.optimization_barrier((target, scalars))
    first, slab, parity, other_parity, *places = scalars
    slab_id = slab.reshape(1).astype(jnp.int32)
    step = 2
    assert lax.axis_size("slab") == 2 and orows == step and ocols % 2 == 0
    cells = orows * ocols * half * lax.axis_size("slab") * strips
    scale = 1.0 / math.sqrt(cells)

    lower = shift_along(volume[:, -1], "slab", 1)
    last = jnp.concatenate([lower[None, :, -1, :], volume[:, :, -1, :].transpose(1, 0, 2)], axis=0)
    left = shift_along(last, "strip", 1)

    w2, wg, ws = vmem_call(
        weights_body,
        (
            sds((outs, 18 * mid), BF16),
            sds((2 * mid, 9 * outs), BF16),
            sds((mid, 27 * channels), BF16),
        ),
        2,
        scalars=1,
    )(slab_id, dilated_weight, strided_weight.T)
    vp, tp = vmem_call(
        split_body,
        (
            sds((pairs, (rows_in + 1) * 9 * channels, lanes), BF16),
            sds((orows, pairs, outs, lanes), BF16),
        ),
        2,
        [VMEM((2, 3, channels * cols_in, half), F32), VMEM((2, outs * ocols, half), F32)],
    )(volume, target)
    vp, hidden, hid_l, hid_r, slope = vmem_call(
        preact_body,
        (
            sds(vp.shape, BF16),
            sds((orows, pairs, mid, lanes), BF16),
            sds((orows, mid, lanes), BF16),
            sds((orows, mid, lanes), BF16),
            sds((orows, pairs, mid, lanes), F32),
        ),
        4,
        [VMEM((3, channels * cols_in, half), F32)],
    )(vp, lower, left, ws)

    from_left = shift_along(hid_r, "strip", 1)
    from_right = shift_along(hid_l, "strip", -1)
    other = swap(hidden)
    other_left = swap(from_left)
    other_right = swap(from_right)

    def forward(*refs):
        forward_body(scale, step, *refs)

    hs, pred, residual = vmem_call(
        forward,
        (
            sds((orows, pairs + 2, 6 * mid, lanes), BF16),
            sds((orows, pairs, outs, lanes), BF16),
            sds((orows, pairs, 3 * outs, lanes), BF16),
        ),
        8,
    )(hidden, from_left, from_right, other, other_left, other_right, w2, tp)

    rows = outs // strips
    half_rows = rows // 2
    mine, send, apart = vmem_call(
        dilated_grad_body,
        (
            sds((strips, half_rows, 9 * mid), F32),
            sds((strips, half_rows, 9 * mid), BF16),
            sds((strips, rows, 9 * mid), BF16),
        ),
        2,
        scalars=1,
    )(slab_id, residual, hs)
    def pick(array, index, dim):
        return lax.dynamic_index_in_dim(array, index, dim, False, allow_negative_indices=False)

    def pair_stage(grad):
        chunks = grad.reshape(groups, 2, *grad.shape[1:])
        got = lax.ppermute(
            pick(chunks, other_parity, 1), "strip", [(i, i ^ 1) for i in range(strips)]
        )
        return pick(chunks, parity, 1).astype(F32) + got.astype(F32)

    def far_stage(grad):
        total = pick(grad, places[0], 0)
        for d in range(1, groups):
            sent = pick(grad, places[d], 0).astype(BF16)
            got = lax.ppermute(sent, "strip", [(i, (i + 2 * d) % strips) for i in range(strips)])
            total = total + got.astype(F32)
        return total

    dg = jnp.concatenate([(mine + swap(send).astype(F32)).astype(BF16), apart], axis=1)
    dg = pair_stage(dg)

    residual, send = lax.optimization_barrier((residual, send))
    gown, ghalo, gother = vmem_call(
        hidden_grad_body,
        (
            sds((orows, pairs, mid, lanes), F32),
            sds((2, orows, mid, lanes), F32),
            sds((pairs + 2, orows, mid, lanes), BF16),
        ),
        2,
    )(residual, wg)

    gx = swap(gother)
    to_left = (ghalo[0] + gx[0].astype(F32)).astype(BF16)
    to_right = (ghalo[1] + gx[-1].astype(F32)).astype(BF16)
    grad_l = shift_along(to_right, "strip", 1)
    grad_r = shift_along(to_left, "strip", -1)

    prediction = vmem_call(
        prediction_body,
        sds((outs, orows, ocols, half), BF16),
        1,
        [VMEM((2, outs * ocols, half), F32)],
    )(pred)
    mid_rows = mid // strips
    width = 9 * mid
    assert width < 27 * channels <= 2 * width
    grad_l, grad_r, dg, prediction = lax.optimization_barrier((grad_l, grad_r, dg, prediction))
    smine, ssend = vmem_call(
        strided_grad_body,
        (sds((strips, mid_rows, width), F32), sds((strips, mid_rows, width), BF16)),
        6,
        scalars=1,
    )(slab_id, gown, gx, grad_l, grad_r, slope, vp)
    sg = pair_stage((smine + swap(ssend).astype(F32)).astype(BF16))
    total = far_stage(jnp.concatenate([dg, sg], axis=1))
    across = swap(total)
    low, high = jnp.where(first, total, across), jnp.where(first, across, total)
    middle = jnp.concatenate([low[:half_rows], high[:half_rows]], axis=0)
    end = half_rows + rows
    dilated_grad = jnp.concatenate([high[half_rows:end], middle, low[half_rows:end]], axis=1)
    strided_grad = jnp.concatenate([low[end:], high[end:, : 27 * channels - width]], axis=1)
    return prediction, strided_grad, dilated_grad


def solution(mesh):
    return jax.shard_map(
        local,
        mesh=mesh,
        in_specs=(P("fold", "slab", "strip", None), P("fold", "slab", "strip", None), P(), P()),
        out_specs=(
            P("fold", "slab", "strip", None),
            P(("fold", "strip"), None),
            P(("fold", "strip"), None),
        ),
        check_vma=False,
    )
```

```python
import math

import jax
import jax.numpy as jnp
from jax import lax
from jax.experimental import pallas as pl
from jax.experimental.pallas import tpu as pltpu
from jax.sharding import PartitionSpec as P


BF16 = jnp.bfloat16
F32 = jnp.float32
VMEM = pltpu.VMEM
VMEM_LIMIT = 20 * 1024 * 1024


def vmem_call(body, out_shape, n_in, scratch=(), scalars=0):
    spec = pl.BlockSpec(memory_space=pltpu.VMEM)
    scalar = pl.BlockSpec(memory_space=pltpu.SMEM)
    return pl.pallas_call(
        body,
        out_shape=out_shape,
        in_specs=[scalar] * scalars + [spec] * n_in,
        out_specs=jax.tree.map(lambda _: spec, out_shape),
        scratch_shapes=list(scratch),
        compiler_params=pltpu.CompilerParams(vmem_limit_bytes=VMEM_LIMIT),
    )


def selection(depth):
    half = depth // 2
    source = lax.broadcasted_iota(jnp.int32, (depth, 3 * half), 0)
    lane = lax.broadcasted_iota(jnp.int32, (depth, 3 * half), 1)
    even = (lane < half) & (source == 2 * lane)
    odd = (lane >= half) & (lane < 2 * half) & (source == 2 * (lane - half) + 1)
    late = (lane >= 2 * half) & (source == 2 * (lane - 2 * half) - 1)
    return jnp.where(even | odd | late, 1.0, 0.0).astype(BF16)


def thirds(values):
    half = values.shape[1] // 3
    return [values[:, k * half : (k + 1) * half] for k in range(3)]


def spread(plane, pick, scratch):
    for k, part in enumerate(thirds(jnp.dot(plane, pick, preferred_element_type=F32))):
        scratch[k] = part


def put_column(vp_ref, values, channels, row, col, pairs):
    half = values[0].shape[1]
    taps = (values[2], values[0], values[1])
    for b in range(3):
        for h in range(2):
            rest = col + 1 - b - 2 * h
            if rest % 4 or not 0 <= rest // 4 < pairs:
                continue
            for c in range(3):
                start = ((row * 3 + b) * 3 + c) * channels
                vp_ref[rest // 4, start : start + channels, h * half : (h + 1) * half] = taps[c]


def split_body(vol_ref, tgt_ref, vp_ref, tp_ref, wide_ref, tall_ref):
    channels, rows, cols, depth = vol_ref.shape
    pairs = cols // 4
    half = depth // 2
    pick = selection(depth)
    for row in range(rows):
        slot = row % 2
        plane = vol_ref[:, row].reshape(channels * cols, depth)
        spread(plane, pick, wide_ref.at[slot])
        for col in range(cols):
            values = [
                wide_ref[slot, k, pl.ds(col, channels, stride=cols), :].astype(BF16)
                for k in range(3)
            ]
            put_column(vp_ref, values, channels, row + 1, col, pairs)
    outs, orows, ocols, _ = tgt_ref.shape
    for row in range(orows):
        slot = row % 2
        tall_ref[slot] = tgt_ref[:, row].astype(F32).reshape(outs * ocols, half)
        for col in range(ocols):
            values = tall_ref[slot, pl.ds(col, outs, stride=ocols), :].astype(BF16)
            tp_ref[row, col // 2, :, (col % 2) * half : (col % 2 + 1) * half] = values


def preact_body(own_ref, hrow_ref, hcol_ref, w_ref, vp_ref, h_ref, hl_ref, hr_ref, slope_ref, wide_ref):
    channels, cols, depth = hrow_ref.shape
    rows_ext = hcol_ref.shape[0]
    orows, pairs, _, _ = h_ref.shape
    vp_ref[:, 9 * channels :] = own_ref[:, 9 * channels :]
    pick = selection(depth)
    spread(hrow_ref[...].reshape(channels * cols, depth), pick, wide_ref)
    for col in range(cols):
        values = [
            wide_ref[k, pl.ds(col, channels, stride=cols), :].astype(BF16) for k in range(3)
        ]
        put_column(vp_ref, values, channels, 0, col, pairs)
    for row in range(rows_ext):
        values = jnp.dot(hcol_ref[row], pick, preferred_element_type=F32).astype(BF16)
        put_column(vp_ref, thirds(values), channels, row, -1, pairs)
    plane = 9 * channels
    for i in range(orows):
        for m in (0, pairs - 1, *range(1, pairs - 1)):
            window = vp_ref[m, 2 * i * plane : (2 * i + 3) * plane, :]
            pre = jnp.dot(w_ref[...], window, preferred_element_type=F32)
            sigma = jax.nn.sigmoid(pre)
            hidden = (pre * sigma).astype(BF16)
            h_ref[i, m] = hidden
            if m == 0:
                hl_ref[i] = hidden
            if m == pairs - 1:
                hr_ref[i] = hidden
            slope_ref[i, m] = sigma * (1.0 + pre * (1.0 - sigma))


def shifted(values, steps):
    half = values.shape[1] // 2
    lane = lax.broadcasted_iota(jnp.int32, (values.shape[0], half), 1)
    keep = lane >= steps if steps > 0 else lane < half + steps
    parts = [
        jnp.where(keep, pltpu.roll(values[:, k * half : (k + 1) * half], steps % half, 1), 0.0)
        for k in range(2)
    ]
    return jnp.concatenate(parts, axis=1)


def weights_body(slab_ref, wd_ref, ws_ref, w2_ref, wg_ref, wst_ref):
    outs, width = wd_ref.shape
    mid = width // 27
    wst_ref[...] = ws_ref[...].T

    def fill(src, a):
        for b in range(3):
            block = (a * 3 + b) * 3 * mid
            to = (b * 2 + src) * 3 * mid
            w2_ref[:, to : to + 3 * mid] = wd_ref[:, block : block + 3 * mid]
            for c in range(3):
                tap = wd_ref[:, block + c * mid : block + (c + 1) * mid]
                column = ((2 - b) * 3 + c) * outs
                wg_ref[src * mid : (src + 1) * mid, column : column + outs] = tap.T

    fill(0, 1)

    @pl.when(slab_ref[0] == 0)
    def _():
        fill(1, 2)

    @pl.when(slab_ref[0] != 0)
    def _():
        fill(1, 0)


NT = (((1,), (1,)), ((), ()))


def put_window(ref, at, tile, base, step):
    mid = tile.shape[0]
    wide = tile.astype(F32)
    ref[(*at, slice(base, base + mid))] = shifted(wide, step).astype(BF16)
    ref[(*at, slice(base + mid, base + 2 * mid))] = tile
    ref[(*at, slice(base + 2 * mid, base + 3 * mid))] = shifted(wide, -step).astype(BF16)


def put_residual(out, target, scale, step, pred_ref, rs_ref, at):
    outs = out.shape[0]
    pred_ref[at] = out.astype(BF16)
    res = ((out - target.astype(F32)) * scale).astype(BF16)
    wide = res.astype(F32)
    rs_ref[(*at, slice(0, outs))] = shifted(wide, -step).astype(BF16)
    rs_ref[(*at, slice(outs, 2 * outs))] = res
    rs_ref[(*at, slice(2 * outs, 3 * outs))] = shifted(wide, step).astype(BF16)


def added(parts):
    total = None
    for part in parts:
        total = part if total is None else total + part
    return total


def inner_body(scale, step, h_ref, o_ref, w2_ref, wg_ref, tp_ref, hs_ref, pred_ref, dg_ref, g_ref, rs_ref):
    orows, pairs, mid, lanes = h_ref.shape
    outs = w2_ref.shape[0]
    block = 3 * outs
    for r in range(orows):
        for x in range(pairs):
            put_window(hs_ref, (r, x), h_ref[r, x], 0, step)
            put_window(hs_ref, (r, x), o_ref[r, x], 3 * mid, step)
    for r in range(orows):
        for m in range(1, pairs - 1):
            window = hs_ref[r, m - 1 : m + 2].reshape(18 * mid, lanes)
            out = jnp.dot(w2_ref[...], window, preferred_element_type=F32)
            put_residual(out, tp_ref[r, m], scale, step, pred_ref, rs_ref, (r, m - 1))
    for b in range(3):
        for src in range(2):
            rows = slice(src * 3 * mid, (src + 1) * 3 * mid)
            to = (b * 2 + src) * 3 * mid
            dg_ref[:, to : to + 3 * mid] = added(
                lax.dot_general(
                    rs_ref[r, m - 1, outs : 2 * outs], hs_ref[r, m - 1 + b, rows], NT,
                    preferred_element_type=F32,
                )
                for r in range(orows)
                for m in range(1, pairs - 1)
            )
    for r in range(orows):
        for x in range(1, pairs + 1):
            low, high = max(x - 2, 1), min(x, pairs - 2)
            first = low - (x - 2)
            window = rs_ref[r, low - 1 : high].reshape((high - low + 1) * block, lanes)
            weights = wg_ref[:, first * block : (first + high - low + 1) * block]
            g_ref[r, x - 1] = jnp.dot(weights, window, preferred_element_type=F32)


def outer_body(
    scale, step, slab_ref, hs_ref, hl_ref, hr_ref, ol_ref, or_ref, w2_ref, tp_ref, dg_ref,
    pred_ref, rs_ref, mine_ref, send_ref, other_ref, edge_ref,
):
    orows, pairs, depth, lanes = hs_ref.shape
    mid = depth // 6
    outs = w2_ref.shape[0]
    ends = (0, pairs - 1)
    for r in range(orows):
        for k, (own, other) in enumerate(((hl_ref, ol_ref), (hr_ref, or_ref))):
            put_window(edge_ref, (r, k), own[r], 0, step)
            put_window(edge_ref, (r, k), other[r], 3 * mid, step)

    def taps(r, m, b):
        x = m - 1 + b
        return edge_ref.at[r, 0] if x < 0 else edge_ref.at[r, 1] if x == pairs else hs_ref.at[r, x]

    for r in range(orows):
        for k, m in enumerate(ends):
            edge = edge_ref[r, k]
            near = hs_ref[r, 0:2] if k == 0 else hs_ref[r, pairs - 2 : pairs]
            near = near.reshape(2 * depth, lanes)
            w_edge = w2_ref[:, :depth] if k == 0 else w2_ref[:, 2 * depth :]
            w_near = w2_ref[:, depth:] if k == 0 else w2_ref[:, : 2 * depth]
            out = jnp.dot(w_edge, edge, preferred_element_type=F32)
            out = out + jnp.dot(w_near, near, preferred_element_type=F32)
            put_residual(out, tp_ref[r, m], scale, step, pred_ref, rs_ref, (r, k))
    for b in range(3):
        columns = slice(b * 3 * mid, (b + 1) * 3 * mid)
        for src in range(2):
            rows = slice(src * 3 * mid, (src + 1) * 3 * mid)
            at = (b * 2 + src) * 3 * mid
            total = dg_ref[:, at : at + 3 * mid] + added(
                lax.dot_general(
                    rs_ref[r, k, outs : 2 * outs], taps(r, m, b)[rows], NT,
                    preferred_element_type=F32,
                )
                for r in range(orows)
                for k, m in enumerate(ends)
            )
            if src == 0:
                split_rows(slab_ref, total, mine_ref, send_ref, columns)
            else:
                strips, count, _ = other_ref.shape
                other_ref[:, :, columns] = total.reshape(strips, count, 3 * mid).astype(BF16)


def hidden_grad_body(rs_ref, wg_ref, g_ref, gown_ref, ghalo_ref, gother_ref):
    orows, _, block, lanes = rs_ref.shape
    pairs, mid = gown_ref.shape[1:3]
    for r in range(orows):
        for x in range(pairs + 2):
            parts = [g_ref[r, x - 1]] if 0 < x <= pairs else []
            for k, m in enumerate((0, pairs - 1)):
                tap = m - (x - 2)
                if 0 <= tap < 3:
                    weights = wg_ref[:, tap * block : (tap + 1) * block]
                    parts.append(jnp.dot(weights, rs_ref[r, k], preferred_element_type=F32))
            grad = added(parts)
            gother_ref[x, r] = grad[mid:].astype(BF16)
            if x == 0:
                ghalo_ref[0, r] = grad[:mid]
            elif x == pairs + 1:
                ghalo_ref[1, r] = grad[:mid]
            else:
                gown_ref[r, x - 1] = grad[:mid]


def split_rows(slab_ref, total, mine_ref, send_ref, columns):
    strips, rows, _ = mine_ref.shape
    parts = total.reshape(strips, 2, rows, total.shape[1])
    first = slab_ref[0] == 0
    mine_ref[:, :, columns] = jnp.where(first, parts[:, 0], parts[:, 1])
    send_ref[:, :, columns] = jnp.where(first, parts[:, 1], parts[:, 0]).astype(BF16)


def strided_part(gown_ref, gx_ref, extra, slope_ref, vp_ref, columns):
    orows = gown_ref.shape[0]
    plane = vp_ref.shape[1] // (2 * orows + 1)

    def part(i, m):
        grad = gown_ref[i, m] + gx_ref[m + 1, i].astype(F32)
        if m in extra:
            grad = grad + extra[m][i].astype(F32)
        pg = (grad * slope_ref[i, m]).astype(BF16)
        window = vp_ref[m, 2 * i * plane : (2 * i + 3) * plane, :]
        return lax.dot_general(pg, window, NT, preferred_element_type=F32)

    return added(part(i, m) for i in range(orows) for m in columns)


def strided_inner_body(gown_ref, gx_ref, slope_ref, vp_ref, sum_ref):
    pairs = gown_ref.shape[1]
    sum_ref[...] = strided_part(gown_ref, gx_ref, {}, slope_ref, vp_ref, range(1, pairs - 1))


def strided_grad_body(
    slab_ref, gown_ref, gx_ref, gl_ref, gr_ref, slope_ref, vp_ref, sum_ref, mine_ref, send_ref
):
    pairs, mid = gown_ref.shape[1:3]
    extra = {0: gl_ref, pairs - 1: gr_ref}
    total = sum_ref[...] + strided_part(
        gown_ref, gx_ref, extra, slope_ref, vp_ref, (0, pairs - 1)
    )
    width = mine_ref.shape[2]
    pad = jnp.zeros((mid, 2 * width - total.shape[1]), F32)
    low, high = total[:, :width], jnp.concatenate([total[:, width:], pad], axis=1)
    first = slab_ref[0] == 0
    mine_ref[...] = jnp.where(first, low, high).reshape(mine_ref.shape)
    send_ref[...] = jnp.where(first, high, low).reshape(mine_ref.shape).astype(BF16)


def prediction_body(inner_ref, outer_ref, out_ref, tall_ref):
    orows, inner, outs, lanes = inner_ref.shape
    half = lanes // 2
    cols = 2 * (inner + 2)
    for r in range(orows):
        slot = r % 2
        for col in range(cols):
            m = col // 2
            tile = outer_ref.at[r, m // (inner + 1)] if m in (0, inner + 1) else inner_ref.at[r, m - 1]
            values = tile[:, (col % 2) * half : (col % 2 + 1) * half]
            tall_ref[slot, pl.ds(col, outs, stride=cols), :] = values.astype(F32)
        out_ref[:, r] = tall_ref[slot].reshape(outs, cols, half).astype(BF16)


def sds(shape, dtype):
    return jax.ShapeDtypeStruct(shape, dtype)


def shift_along(value, axis, steps):
    count = lax.axis_size(axis)
    pairs = [(i, i + steps) for i in range(count) if 0 <= i + steps < count]
    return lax.ppermute(value, axis, pairs)


def swap(value):
    return lax.ppermute(value, "slab", [(0, 1), (1, 0)])


def local(volume, target, strided_weight, dilated_weight):
    channels, rows_in, cols_in, depth = volume.shape
    mid = strided_weight.shape[0]
    outs = dilated_weight.shape[0]
    orows, ocols, half = rows_in // 2, cols_in // 2, depth // 2
    pairs, lanes = ocols // 2, 2 * half
    strips = lax.axis_size("strip")
    slab = lax.axis_index("slab")
    strip = lax.axis_index("strip")
    groups = strips // 2
    place, parity = strip // 2, strip % 2
    scalars = (slab == 0, slab, parity, 1 - parity, *((place + d) % groups for d in range(groups)))
    target, scalars = lax.optimization_barrier((target, scalars))
    first, slab, parity, other_parity, *places = scalars
    slab_id = slab.reshape(1).astype(jnp.int32)
    step = 2
    assert lax.axis_size("slab") == 2 and orows == step and ocols % 2 == 0
    cells = orows * ocols * half * lax.axis_size("slab") * strips
    scale = 1.0 / math.sqrt(cells)

    lower = shift_along(volume[:, -1], "slab", 1)
    last = jnp.concatenate([lower[None, :, -1, :], volume[:, :, -1, :].transpose(1, 0, 2)], axis=0)
    left = shift_along(last, "strip", 1)

    w2, wg, ws = vmem_call(
        weights_body,
        (
            sds((outs, 18 * mid), BF16),
            sds((2 * mid, 9 * outs), BF16),
            sds((mid, 27 * channels), BF16),
        ),
        2,
        scalars=1,
    )(slab_id, dilated_weight, strided_weight.T)
    vp, tp = vmem_call(
        split_body,
        (
            sds((pairs, (rows_in + 1) * 9 * channels, lanes), BF16),
            sds((orows, pairs, outs, lanes), BF16),
        ),
        2,
        [VMEM((2, 3, channels * cols_in, half), F32), VMEM((2, outs * ocols, half), F32)],
    )(volume, target)
    vp, hidden, hid_l, hid_r, slope = vmem_call(
        preact_body,
        (
            sds(vp.shape, BF16),
            sds((orows, pairs, mid, lanes), BF16),
            sds((orows, mid, lanes), BF16),
            sds((orows, mid, lanes), BF16),
            sds((orows, pairs, mid, lanes), F32),
        ),
        4,
        [VMEM((3, channels * cols_in, half), F32)],
    )(vp, lower, left, ws)

    from_left = shift_along(hid_r, "strip", 1)
    from_right = shift_along(hid_l, "strip", -1)
    other = swap(hidden)

    def inner(*refs):
        inner_body(scale, step, *refs)

    def outer(*refs):
        outer_body(scale, step, *refs)

    hs, pred_in, dg_in, g_in = vmem_call(
        inner,
        (
            sds((orows, pairs, 6 * mid, lanes), BF16),
            sds((orows, pairs - 2, outs, lanes), BF16),
            sds((outs, 18 * mid), F32),
            sds((orows, pairs, 2 * mid, lanes), F32),
        ),
        5,
        [VMEM((orows, pairs - 2, 3 * outs, lanes), BF16)],
    )(hidden, other, w2, wg, tp)

    from_left, from_right, hs = lax.optimization_barrier((from_left, from_right, hs))
    other_left = swap(from_left)
    other_right = swap(from_right)

    rows = outs // strips
    half_rows = rows // 2
    pred_out, residual, mine, send, apart = vmem_call(
        outer,
        (
            sds((orows, 2, outs, lanes), BF16),
            sds((orows, 2, 3 * outs, lanes), BF16),
            sds((strips, half_rows, 9 * mid), F32),
            sds((strips, half_rows, 9 * mid), BF16),
            sds((strips, rows, 9 * mid), BF16),
        ),
        8,
        [VMEM((orows, 2, 6 * mid, lanes), BF16)],
        scalars=1,
    )(slab_id, hs, from_left, from_right, other_left, other_right, w2, tp, dg_in)

    def pick(array, index, dim):
        return lax.dynamic_index_in_dim(array, index, dim, False, allow_negative_indices=False)

    def pair_stage(grad):
        chunks = grad.reshape(groups, 2, *grad.shape[1:])
        got = lax.ppermute(
            pick(chunks, other_parity, 1), "strip", [(i, i ^ 1) for i in range(strips)]
        )
        return pick(chunks, parity, 1).astype(F32), got

    def far_stage(grad):
        total = pick(grad, places[0], 0)
        for d in range(1, groups):
            sent = pick(grad, places[d], 0).astype(BF16)
            got = lax.ppermute(sent, "strip", [(i, (i + 2 * d) % strips) for i in range(strips)])
            total = total + got.astype(F32)
        return total

    dg = jnp.concatenate([(mine + swap(send).astype(F32)).astype(BF16), apart], axis=1)
    dg, dg_got = pair_stage(dg)

    residual, send = lax.optimization_barrier((residual, send))
    gown, ghalo, gother = vmem_call(
        hidden_grad_body,
        (
            sds((orows, pairs, mid, lanes), F32),
            sds((2, orows, mid, lanes), F32),
            sds((pairs + 2, orows, mid, lanes), BF16),
        ),
        3,
    )(residual, wg, g_in)

    gx = swap(gother)
    to_left = (ghalo[0] + gx[0].astype(F32)).astype(BF16)
    to_right = (ghalo[1] + gx[-1].astype(F32)).astype(BF16)
    grad_l = shift_along(to_right, "strip", 1)
    grad_r = shift_along(to_left, "strip", -1)

    prediction = vmem_call(
        prediction_body,
        sds((outs, orows, ocols, half), BF16),
        2,
        [VMEM((2, outs * ocols, half), F32)],
    )(pred_in, pred_out)
    sg_in = vmem_call(strided_inner_body, sds((mid, 27 * channels), F32), 4)(gown, gx, slope, vp)
    mid_rows = mid // strips
    width = 9 * mid
    assert width < 27 * channels <= 2 * width
    grad_l, grad_r, dg_got, prediction, sg_in = lax.optimization_barrier(
        (grad_l, grad_r, dg_got, prediction, sg_in)
    )
    dg = dg + dg_got.astype(F32)
    smine, ssend = vmem_call(
        strided_grad_body,
        (sds((strips, mid_rows, width), F32), sds((strips, mid_rows, width), BF16)),
        7,
        scalars=1,
    )(slab_id, gown, gx, grad_l, grad_r, slope, vp, sg_in)
    sg, sg_got = pair_stage((smine + swap(ssend).astype(F32)).astype(BF16))
    sg = sg + sg_got.astype(F32)
    total = far_stage(jnp.concatenate([dg, sg], axis=1))
    across = swap(total)
    low, high = jnp.where(first, total, across), jnp.where(first, across, total)
    middle = jnp.concatenate([low[:half_rows], high[:half_rows]], axis=0)
    end = half_rows + rows
    dilated_grad = jnp.concatenate([high[half_rows:end], middle, low[half_rows:end]], axis=1)
    strided_grad = jnp.concatenate([low[end:], high[end:, : 27 * channels - width]], axis=1)
    return prediction, strided_grad, dilated_grad


def solution(mesh):
    return jax.shard_map(
        local,
        mesh=mesh,
        in_specs=(P("fold", "slab", "strip", None), P("fold", "slab", "strip", None), P(), P()),
        out_specs=(
            P("fold", "slab", "strip", None),
            P(("fold", "strip"), None),
            P(("fold", "strip"), None),
        ),
        check_vma=False,
    )
```

```python
import math

import jax
import jax.numpy as jnp
from jax import lax
from jax.experimental import pallas as pl
from jax.experimental.pallas import tpu as pltpu
from jax.sharding import PartitionSpec as P


BF16 = jnp.bfloat16
F32 = jnp.float32
VMEM = pltpu.VMEM
VMEM_LIMIT = 20 * 1024 * 1024


def vmem_call(body, out_shape, n_in, scratch=(), scalars=0):
    spec = pl.BlockSpec(memory_space=pltpu.VMEM)
    scalar = pl.BlockSpec(memory_space=pltpu.SMEM)
    return pl.pallas_call(
        body,
        out_shape=out_shape,
        in_specs=[scalar] * scalars + [spec] * n_in,
        out_specs=jax.tree.map(lambda _: spec, out_shape),
        scratch_shapes=list(scratch),
        compiler_params=pltpu.CompilerParams(vmem_limit_bytes=VMEM_LIMIT),
    )


def selection(depth):
    half = depth // 2
    source = lax.broadcasted_iota(jnp.int32, (depth, 3 * half), 0)
    lane = lax.broadcasted_iota(jnp.int32, (depth, 3 * half), 1)
    even = (lane < half) & (source == 2 * lane)
    odd = (lane >= half) & (lane < 2 * half) & (source == 2 * (lane - half) + 1)
    late = (lane >= 2 * half) & (source == 2 * (lane - 2 * half) - 1)
    return jnp.where(even | odd | late, 1.0, 0.0).astype(BF16)


def thirds(values):
    half = values.shape[1] // 3
    return [values[:, k * half : (k + 1) * half] for k in range(3)]


def spread(plane, pick, scratch):
    for k, part in enumerate(thirds(jnp.dot(plane, pick, preferred_element_type=F32))):
        scratch[k] = part


def put_column(vp_ref, values, channels, row, col, pairs):
    half = values[0].shape[1]
    taps = (values[2], values[0], values[1])
    for b in range(3):
        for h in range(2):
            rest = col + 1 - b - 2 * h
            if rest % 4 or not 0 <= rest // 4 < pairs:
                continue
            for c in range(3):
                start = ((row * 3 + b) * 3 + c) * channels
                vp_ref[rest // 4, start : start + channels, h * half : (h + 1) * half] = taps[c]


def split_body(vol_ref, tgt_ref, vp_ref, tp_ref, wide_ref, tall_ref):
    channels, rows, cols, depth = vol_ref.shape
    pairs = cols // 4
    half = depth // 2
    pick = selection(depth)
    for row in range(rows):
        slot = row % 2
        plane = vol_ref[:, row].reshape(channels * cols, depth)
        spread(plane, pick, wide_ref.at[slot])
        for col in range(cols):
            values = [
                wide_ref[slot, k, pl.ds(col, channels, stride=cols), :].astype(BF16)
                for k in range(3)
            ]
            put_column(vp_ref, values, channels, row + 1, col, pairs)
    outs, orows, ocols, _ = tgt_ref.shape
    for row in range(orows):
        slot = row % 2
        tall_ref[slot] = tgt_ref[:, row].astype(F32).reshape(outs * ocols, half)
        for col in range(ocols):
            values = tall_ref[slot, pl.ds(col, outs, stride=ocols), :].astype(BF16)
            tp_ref[row, col // 2, :, (col % 2) * half : (col % 2 + 1) * half] = values


def preact_body(own_ref, hrow_ref, hcol_ref, w_ref, vp_ref, h_ref, hl_ref, hr_ref, slope_ref, wide_ref):
    channels, cols, depth = hrow_ref.shape
    rows_ext = hcol_ref.shape[0]
    orows, pairs, _, _ = h_ref.shape
    vp_ref[:, 9 * channels :] = own_ref[:, 9 * channels :]
    pick = selection(depth)
    spread(hrow_ref[...].reshape(channels * cols, depth), pick, wide_ref)
    for col in range(cols):
        values = [
            wide_ref[k, pl.ds(col, channels, stride=cols), :].astype(BF16) for k in range(3)
        ]
        put_column(vp_ref, values, channels, 0, col, pairs)
    for row in range(rows_ext):
        values = jnp.dot(hcol_ref[row], pick, preferred_element_type=F32).astype(BF16)
        put_column(vp_ref, thirds(values), channels, row, -1, pairs)
    plane = 9 * channels
    for i in range(orows):
        for m in (0, pairs - 1, *range(1, pairs - 1)):
            window = vp_ref[m, 2 * i * plane : (2 * i + 3) * plane, :]
            pre = jnp.dot(w_ref[...], window, preferred_element_type=F32)
            sigma = jax.nn.sigmoid(pre)
            hidden = (pre * sigma).astype(BF16)
            h_ref[i, m] = hidden
            if m == 0:
                hl_ref[i] = hidden
            if m == pairs - 1:
                hr_ref[i] = hidden
            slope_ref[i, m] = sigma * (1.0 + pre * (1.0 - sigma))


def shifted(values, steps):
    half = values.shape[1] // 2
    lane = lax.broadcasted_iota(jnp.int32, (values.shape[0], half), 1)
    keep = lane >= steps if steps > 0 else lane < half + steps
    parts = [
        jnp.where(keep, pltpu.roll(values[:, k * half : (k + 1) * half], steps % half, 1), 0.0)
        for k in range(2)
    ]
    return jnp.concatenate(parts, axis=1)


def weights_body(slab_ref, wd_ref, ws_ref, w2_ref, wg_ref, wst_ref):
    outs, width = wd_ref.shape
    mid = width // 27
    wst_ref[...] = ws_ref[...].T

    def fill(src, a):
        for b in range(3):
            block = (a * 3 + b) * 3 * mid
            to = (b * 2 + src) * 3 * mid
            w2_ref[:, to : to + 3 * mid] = wd_ref[:, block : block + 3 * mid]
            for c in range(3):
                tap = wd_ref[:, block + c * mid : block + (c + 1) * mid]
                column = ((2 - b) * 3 + c) * outs
                wg_ref[src * mid : (src + 1) * mid, column : column + outs] = tap.T

    fill(0, 1)

    @pl.when(slab_ref[0] == 0)
    def _():
        fill(1, 2)

    @pl.when(slab_ref[0] != 0)
    def _():
        fill(1, 0)


NT = (((1,), (1,)), ((), ()))


def put_window(ref, at, tile, base, step):
    mid = tile.shape[0]
    wide = tile.astype(F32)
    ref[(*at, slice(base, base + mid))] = shifted(wide, step).astype(BF16)
    ref[(*at, slice(base + mid, base + 2 * mid))] = tile
    ref[(*at, slice(base + 2 * mid, base + 3 * mid))] = shifted(wide, -step).astype(BF16)


def put_residual(out, target, scale, step, pred_ref, rs_ref, at):
    outs = out.shape[0]
    pred_ref[at] = out.astype(BF16)
    res = ((out - target.astype(F32)) * scale).astype(BF16)
    wide = res.astype(F32)
    rs_ref[(*at, slice(0, outs))] = shifted(wide, -step).astype(BF16)
    rs_ref[(*at, slice(outs, 2 * outs))] = res
    rs_ref[(*at, slice(2 * outs, 3 * outs))] = shifted(wide, step).astype(BF16)


def added(parts):
    total = None
    for part in parts:
        total = part if total is None else total + part
    return total


def inner_body(scale, step, h_ref, o_ref, w2_ref, wg_ref, tp_ref, hs_ref, pred_ref, dg_ref, g_ref, rs_ref):
    orows, pairs, mid, lanes = h_ref.shape
    outs = w2_ref.shape[0]
    block = 3 * outs
    for r in range(orows):
        for x in range(pairs):
            put_window(hs_ref, (r, x), h_ref[r, x], 0, step)
            put_window(hs_ref, (r, x), o_ref[r, x], 3 * mid, step)
    for r in range(orows):
        for m in range(1, pairs - 1):
            window = hs_ref[r, m - 1 : m + 2].reshape(18 * mid, lanes)
            out = jnp.dot(w2_ref[...], window, preferred_element_type=F32)
            put_residual(out, tp_ref[r, m], scale, step, pred_ref, rs_ref, (r, m - 1))
    for b in range(3):
        for src in range(2):
            rows = slice(src * 3 * mid, (src + 1) * 3 * mid)
            to = (b * 2 + src) * 3 * mid
            dg_ref[:, to : to + 3 * mid] = added(
                lax.dot_general(
                    rs_ref[r, m - 1, outs : 2 * outs], hs_ref[r, m - 1 + b, rows], NT,
                    preferred_element_type=F32,
                )
                for r in range(orows)
                for m in range(1, pairs - 1)
            )
    for r in range(orows):
        for x in range(1, pairs + 1):
            low, high = max(x - 2, 1), min(x, pairs - 2)
            first = low - (x - 2)
            window = rs_ref[r, low - 1 : high].reshape((high - low + 1) * block, lanes)
            weights = wg_ref[:, first * block : (first + high - low + 1) * block]
            g_ref[r, x - 1] = jnp.dot(weights, window, preferred_element_type=F32)


def outer_body(
    scale, step, slab_ref, hs_ref, hl_ref, hr_ref, ol_ref, or_ref, w2_ref, tp_ref, dg_ref,
    pred_ref, rs_ref, mine_ref, send_ref, other_ref, edge_ref,
):
    orows, pairs, depth, lanes = hs_ref.shape
    mid = depth // 6
    outs = w2_ref.shape[0]
    ends = (0, pairs - 1)
    for r in range(orows):
        for k, (own, other) in enumerate(((hl_ref, ol_ref), (hr_ref, or_ref))):
            put_window(edge_ref, (r, k), own[r], 0, step)
            put_window(edge_ref, (r, k), other[r], 3 * mid, step)

    def taps(r, m, b):
        x = m - 1 + b
        return edge_ref.at[r, 0] if x < 0 else edge_ref.at[r, 1] if x == pairs else hs_ref.at[r, x]

    for r in range(orows):
        for k, m in enumerate(ends):
            edge = edge_ref[r, k]
            near = hs_ref[r, 0:2] if k == 0 else hs_ref[r, pairs - 2 : pairs]
            near = near.reshape(2 * depth, lanes)
            w_edge = w2_ref[:, :depth] if k == 0 else w2_ref[:, 2 * depth :]
            w_near = w2_ref[:, depth:] if k == 0 else w2_ref[:, : 2 * depth]
            out = jnp.dot(w_edge, edge, preferred_element_type=F32)
            out = out + jnp.dot(w_near, near, preferred_element_type=F32)
            put_residual(out, tp_ref[r, m], scale, step, pred_ref, rs_ref, (r, k))
    for b in range(3):
        columns = slice(b * 3 * mid, (b + 1) * 3 * mid)
        for src in range(2):
            rows = slice(src * 3 * mid, (src + 1) * 3 * mid)
            at = (b * 2 + src) * 3 * mid
            total = dg_ref[:, at : at + 3 * mid] + added(
                lax.dot_general(
                    rs_ref[r, k, outs : 2 * outs], taps(r, m, b)[rows], NT,
                    preferred_element_type=F32,
                )
                for r in range(orows)
                for k, m in enumerate(ends)
            )
            if src == 0:
                split_rows(slab_ref, total, mine_ref, send_ref, columns)
            else:
                strips, count, _ = other_ref.shape
                other_ref[:, :, columns] = total.reshape(strips, count, 3 * mid).astype(BF16)


def hidden_grad_body(rs_ref, wg_ref, g_ref, gown_ref, ghalo_ref, gother_ref):
    orows, _, block, lanes = rs_ref.shape
    pairs, mid = gown_ref.shape[1:3]
    for r in range(orows):
        for x in range(pairs + 2):
            parts = [g_ref[r, x - 1]] if 0 < x <= pairs else []
            for k, m in enumerate((0, pairs - 1)):
                tap = m - (x - 2)
                if 0 <= tap < 3:
                    weights = wg_ref[:, tap * block : (tap + 1) * block]
                    parts.append(jnp.dot(weights, rs_ref[r, k], preferred_element_type=F32))
            grad = added(parts)
            gother_ref[x, r] = grad[mid:].astype(BF16)
            if x == 0:
                ghalo_ref[0, r] = grad[:mid]
            elif x == pairs + 1:
                ghalo_ref[1, r] = grad[:mid]
            else:
                gown_ref[r, x - 1] = grad[:mid]


def split_rows(slab_ref, total, mine_ref, send_ref, columns):
    strips, rows, _ = mine_ref.shape
    parts = total.reshape(strips, 2, rows, total.shape[1])
    first = slab_ref[0] == 0
    mine_ref[:, :, columns] = jnp.where(first, parts[:, 0], parts[:, 1])
    send_ref[:, :, columns] = jnp.where(first, parts[:, 1], parts[:, 0]).astype(BF16)


def strided_part(gown_ref, gx_ref, extra, slope_ref, vp_ref, columns):
    orows = gown_ref.shape[0]
    plane = vp_ref.shape[1] // (2 * orows + 1)

    def part(i, m):
        grad = gown_ref[i, m] + gx_ref[m + 1, i].astype(F32)
        if m in extra:
            grad = grad + extra[m][i].astype(F32)
        pg = (grad * slope_ref[i, m]).astype(BF16)
        window = vp_ref[m, 2 * i * plane : (2 * i + 3) * plane, :]
        return lax.dot_general(pg, window, NT, preferred_element_type=F32)

    return added(part(i, m) for i in range(orows) for m in columns)


def strided_inner_body(gown_ref, gx_ref, slope_ref, vp_ref, sum_ref):
    pairs = gown_ref.shape[1]
    sum_ref[...] = strided_part(gown_ref, gx_ref, {}, slope_ref, vp_ref, range(1, pairs - 1))


def strided_grad_body(
    slab_ref, gown_ref, gx_ref, gl_ref, gr_ref, slope_ref, vp_ref, sum_ref, mine_ref, send_ref
):
    pairs, mid = gown_ref.shape[1:3]
    extra = {0: gl_ref, pairs - 1: gr_ref}
    total = sum_ref[...] + strided_part(
        gown_ref, gx_ref, extra, slope_ref, vp_ref, (0, pairs - 1)
    )
    width = mine_ref.shape[2]
    pad = jnp.zeros((mid, 2 * width - total.shape[1]), F32)
    low, high = total[:, :width], jnp.concatenate([total[:, width:], pad], axis=1)
    first = slab_ref[0] == 0
    mine_ref[...] = jnp.where(first, low, high).reshape(mine_ref.shape)
    send_ref[...] = jnp.where(first, high, low).reshape(mine_ref.shape).astype(BF16)


def prediction_body(inner_ref, outer_ref, out_ref, tall_ref):
    orows, inner, outs, lanes = inner_ref.shape
    half = lanes // 2
    cols = 2 * (inner + 2)
    for r in range(orows):
        slot = r % 2
        for col in range(cols):
            m = col // 2
            tile = outer_ref.at[r, m // (inner + 1)] if m in (0, inner + 1) else inner_ref.at[r, m - 1]
            values = tile[:, (col % 2) * half : (col % 2 + 1) * half]
            tall_ref[slot, pl.ds(col, outs, stride=cols), :] = values.astype(F32)
        out_ref[:, r] = tall_ref[slot].reshape(outs, cols, half).astype(BF16)


def sds(shape, dtype):
    return jax.ShapeDtypeStruct(shape, dtype)


def shift_along(value, axis, steps):
    count = lax.axis_size(axis)
    pairs = [(i, i + steps) for i in range(count) if 0 <= i + steps < count]
    return lax.ppermute(value, axis, pairs)


def swap(value):
    return lax.ppermute(value, "slab", [(0, 1), (1, 0)])


def local(volume, target, strided_weight, dilated_weight):
    channels, rows_in, cols_in, depth = volume.shape
    mid = strided_weight.shape[0]
    outs = dilated_weight.shape[0]
    orows, ocols, half = rows_in // 2, cols_in // 2, depth // 2
    pairs, lanes = ocols // 2, 2 * half
    strips = lax.axis_size("strip")
    slab = lax.axis_index("slab")
    strip = lax.axis_index("strip")
    groups = strips // 2
    place, parity = strip // 2, strip % 2
    scalars = (slab == 0, slab, parity, 1 - parity, *((place + d) % groups for d in range(groups)))
    target, scalars = lax.optimization_barrier((target, scalars))
    first, slab, parity, other_parity, *places = scalars
    slab_id = slab.reshape(1).astype(jnp.int32)
    step = 2
    assert lax.axis_size("slab") == 2 and orows == step and ocols % 2 == 0
    cells = orows * ocols * half * lax.axis_size("slab") * strips
    scale = 1.0 / math.sqrt(cells)

    lower = shift_along(volume[:, -1], "slab", 1)
    last = jnp.concatenate([lower[None, :, -1, :], volume[:, :, -1, :].transpose(1, 0, 2)], axis=0)
    left = shift_along(last, "strip", 1)

    w2, wg, ws = vmem_call(
        weights_body,
        (
            sds((outs, 18 * mid), BF16),
            sds((2 * mid, 9 * outs), BF16),
            sds((mid, 27 * channels), BF16),
        ),
        2,
        scalars=1,
    )(slab_id, dilated_weight, strided_weight.T)
    vp, tp = vmem_call(
        split_body,
        (
            sds((pairs, (rows_in + 1) * 9 * channels, lanes), BF16),
            sds((orows, pairs, outs, lanes), BF16),
        ),
        2,
        [VMEM((2, 3, channels * cols_in, half), F32), VMEM((2, outs * ocols, half), F32)],
    )(volume, target)
    vp, hidden, hid_l, hid_r, slope = vmem_call(
        preact_body,
        (
            sds(vp.shape, BF16),
            sds((orows, pairs, mid, lanes), BF16),
            sds((orows, mid, lanes), BF16),
            sds((orows, mid, lanes), BF16),
            sds((orows, pairs, mid, lanes), F32),
        ),
        4,
        [VMEM((3, channels * cols_in, half), F32)],
    )(vp, lower, left, ws)

    from_left = shift_along(hid_r, "strip", 1)
    from_right = shift_along(hid_l, "strip", -1)
    other = swap(hidden)

    def inner(*refs):
        inner_body(scale, step, *refs)

    def outer(*refs):
        outer_body(scale, step, *refs)

    hs, pred_in, dg_in, g_in = vmem_call(
        inner,
        (
            sds((orows, pairs, 6 * mid, lanes), BF16),
            sds((orows, pairs - 2, outs, lanes), BF16),
            sds((outs, 18 * mid), F32),
            sds((orows, pairs, 2 * mid, lanes), F32),
        ),
        5,
        [VMEM((orows, pairs - 2, 3 * outs, lanes), BF16)],
    )(hidden, other, w2, wg, tp)

    from_left, from_right, hs = lax.optimization_barrier((from_left, from_right, hs))
    other_left = swap(from_left)
    other_right = swap(from_right)

    rows = outs // strips
    half_rows = rows // 2
    pred_out, residual, mine, send, apart = vmem_call(
        outer,
        (
            sds((orows, 2, outs, lanes), BF16),
            sds((orows, 2, 3 * outs, lanes), BF16),
            sds((strips, half_rows, 9 * mid), F32),
            sds((strips, half_rows, 9 * mid), BF16),
            sds((strips, rows, 9 * mid), BF16),
        ),
        8,
        [VMEM((orows, 2, 6 * mid, lanes), BF16)],
        scalars=1,
    )(slab_id, hs, from_left, from_right, other_left, other_right, w2, tp, dg_in)

    def pick(array, index, dim):
        return lax.dynamic_index_in_dim(array, index, dim, False, allow_negative_indices=False)

    def pair_swap(value):
        return lax.ppermute(value, "strip", [(i, i ^ 1) for i in range(strips)])

    def far_swap(chunks):
        return [
            lax.ppermute(
                pick(chunks, places[d], 0).astype(BF16),
                "strip",
                [(i, (i + 2 * d) % strips) for i in range(strips)],
            )
            for d in range(1, groups)
        ]

    def far_sum(chunks, got):
        return added([pick(chunks, places[0], 0).astype(F32), *(g.astype(F32) for g in got)])

    apart = apart.reshape(groups, 2, rows, 9 * mid)
    apart_got = pair_swap(pick(apart, other_parity, 1))
    dg_own = (mine + swap(send).astype(F32)).astype(BF16)

    send, residual = lax.optimization_barrier((send, residual))
    gown, ghalo, gother = vmem_call(
        hidden_grad_body,
        (
            sds((orows, pairs, mid, lanes), F32),
            sds((2, orows, mid, lanes), F32),
            sds((pairs + 2, orows, mid, lanes), BF16),
        ),
        3,
    )(residual, wg, g_in)

    gx = swap(gother)
    to_left = (ghalo[0] + gx[0].astype(F32)).astype(BF16)
    to_right = (ghalo[1] + gx[-1].astype(F32)).astype(BF16)
    grad_l = shift_along(to_right, "strip", 1)
    grad_r = shift_along(to_left, "strip", -1)

    prediction = vmem_call(
        prediction_body,
        sds((outs, orows, ocols, half), BF16),
        2,
        [VMEM((2, outs * ocols, half), F32)],
    )(pred_in, pred_out)
    sg_in = vmem_call(strided_inner_body, sds((mid, 27 * channels), F32), 4)(gown, gx, slope, vp)
    mid_rows = mid // strips
    width = 9 * mid
    assert width < 27 * channels <= 2 * width
    dg_own, prediction = lax.optimization_barrier((dg_own, prediction))
    dg_own = dg_own.reshape(groups, 2, half_rows, 9 * mid)
    own_got = far_swap(dg_own)
    grad_l, grad_r, apart_got, sg_in = lax.optimization_barrier((grad_l, grad_r, apart_got, sg_in))
    smine, ssend = vmem_call(
        strided_grad_body,
        (sds((strips, mid_rows, width), F32), sds((strips, mid_rows, width), BF16)),
        7,
        scalars=1,
    )(slab_id, gown, gx, grad_l, grad_r, slope, vp, sg_in)
    sg = (smine + swap(ssend).astype(F32)).astype(BF16).reshape(groups, 2, mid_rows, width)
    own = far_sum(dg_own, own_got)
    sent = jnp.concatenate(
        [
            pick(sg, other_parity, 1).reshape(groups * mid_rows, width),
            pick(own, other_parity, 0).astype(BF16),
        ],
        axis=0,
    )
    got = pair_swap(sent).astype(F32)
    own = pick(own, parity, 0) + got[groups * mid_rows :]
    sg = pick(sg, parity, 1).astype(F32) + got[: groups * mid_rows].reshape(groups, mid_rows, width)
    dg = pick(apart, parity, 1).astype(F32) + apart_got.astype(F32)
    total = jnp.concatenate([dg, sg], axis=1)
    total = jnp.concatenate([own, far_sum(total, far_swap(total))], axis=0)
    across = swap(total)
    low, high = jnp.where(first, total, across), jnp.where(first, across, total)
    middle = jnp.concatenate([low[:half_rows], high[:half_rows]], axis=0)
    end = half_rows + rows
    dilated_grad = jnp.concatenate([high[half_rows:end], middle, low[half_rows:end]], axis=1)
    strided_grad = jnp.concatenate([low[end:], high[end:, : 27 * channels - width]], axis=1)
    return prediction, strided_grad, dilated_grad


def solution(mesh):
    return jax.shard_map(
        local,
        mesh=mesh,
        in_specs=(P("fold", "slab", "strip", None), P("fold", "slab", "strip", None), P(), P()),
        out_specs=(
            P("fold", "slab", "strip", None),
            P(("fold", "strip"), None),
            P(("fold", "strip"), None),
        ),
        check_vma=False,
    )
```

```python
import math

import jax
import jax.numpy as jnp
from jax import lax
from jax.experimental import pallas as pl
from jax.experimental.pallas import tpu as pltpu
from jax.sharding import PartitionSpec as P


BF16 = jnp.bfloat16
F32 = jnp.float32
VMEM = pltpu.VMEM
VMEM_LIMIT = 20 * 1024 * 1024


def vmem_call(body, out_shape, n_in, scratch=(), scalars=0, in_hbm=0):
    spec = pl.BlockSpec(memory_space=pltpu.VMEM)
    scalar = pl.BlockSpec(memory_space=pltpu.SMEM)
    hbm = pl.BlockSpec(memory_space=pltpu.HBM)
    return pl.pallas_call(
        body,
        out_shape=out_shape,
        in_specs=[scalar] * scalars + [hbm] * in_hbm + [spec] * n_in,
        out_specs=jax.tree.map(lambda _: spec, out_shape),
        scratch_shapes=list(scratch),
        compiler_params=pltpu.CompilerParams(vmem_limit_bytes=VMEM_LIMIT),
    )


def selection(depth):
    half = depth // 2
    source = lax.broadcasted_iota(jnp.int32, (depth, 3 * half), 0)
    lane = lax.broadcasted_iota(jnp.int32, (depth, 3 * half), 1)
    even = (lane < half) & (source == 2 * lane)
    odd = (lane >= half) & (lane < 2 * half) & (source == 2 * (lane - half) + 1)
    late = (lane >= 2 * half) & (source == 2 * (lane - 2 * half) - 1)
    return jnp.where(even | odd | late, 1.0, 0.0).astype(BF16)


def thirds(values):
    half = values.shape[1] // 3
    return [values[:, k * half : (k + 1) * half] for k in range(3)]


def spread(plane, pick, scratch):
    for k, part in enumerate(thirds(jnp.dot(plane, pick, preferred_element_type=F32))):
        scratch[k] = part


def put_column(vp_ref, values, channels, row, col, pairs):
    half = values[0].shape[1]
    taps = (values[2], values[0], values[1])
    for b in range(3):
        for h in range(2):
            rest = col + 1 - b - 2 * h
            if rest % 4 or not 0 <= rest // 4 < pairs:
                continue
            for c in range(3):
                start = ((row * 3 + b) * 3 + c) * channels
                vp_ref[rest // 4, start : start + channels, h * half : (h + 1) * half] = taps[c]


def edge_body(vol_ref, edge_ref, half_ref, sem):
    channels, rows, cols, depth = vol_ref.shape
    count = half_ref.shape[2]
    copy = pltpu.make_async_copy(vol_ref.at[:, :, cols - count :], half_ref, sem)
    copy.start()
    channel = lax.broadcasted_iota(jnp.int32, (channels, channels * count), 0)
    source = lax.broadcasted_iota(jnp.int32, (channels, channels * count), 1)
    last = jnp.where(source == channel * count + count - 1, 1.0, 0.0).astype(BF16)
    copy.wait()
    for row in range(rows):
        plane = half_ref[:, row].astype(F32).reshape(channels * count, depth).astype(BF16)
        edge_ref[row] = jnp.dot(last, plane, preferred_element_type=F32).astype(BF16)


def split_body(vol_ref, vp_ref, last_ref, wide_ref):
    channels, rows, cols, depth = vol_ref.shape
    pairs = cols // 4
    pick = selection(depth)
    for row in range(rows):
        slot = row % 2
        plane = vol_ref[:, row].reshape(channels * cols, depth)
        if row == rows - 1:
            last_ref[...] = plane
        spread(plane, pick, wide_ref.at[slot])
        for col in range(cols):
            values = [
                wide_ref[slot, k, pl.ds(col, channels, stride=cols), :].astype(BF16)
                for k in range(3)
            ]
            put_column(vp_ref, values, channels, row + 1, col, pairs)


def target_body(tgt_ref, tp_ref, tall_ref):
    outs, orows, ocols, half = tgt_ref.shape
    for row in range(orows):
        slot = row % 2
        tall_ref[slot] = tgt_ref[:, row].astype(F32).reshape(outs * ocols, half)
        for col in range(ocols):
            values = tall_ref[slot, pl.ds(col, outs, stride=ocols), :].astype(BF16)
            tp_ref[row, col // 2, :, (col % 2) * half : (col % 2 + 1) * half] = values


def preact_body(own_ref, hrow_ref, hcol_ref, w_ref, vp_ref, h_ref, hl_ref, hr_ref, slope_ref, wide_ref):
    rows_in, channels, depth = hcol_ref.shape
    size = hrow_ref.shape[0] - channels
    cols = size // channels
    orows, pairs, _, _ = h_ref.shape
    vp_ref[:, 9 * channels :] = own_ref[:, 9 * channels :]
    pick = selection(depth)
    spread(hrow_ref[:size], pick, wide_ref)
    for col in range(cols):
        values = [
            wide_ref[k, pl.ds(col, channels, stride=cols), :].astype(BF16) for k in range(3)
        ]
        put_column(vp_ref, values, channels, 0, col, pairs)
    for row in range(rows_in + 1):
        plane = hrow_ref[size:] if row == 0 else hcol_ref[row - 1]
        values = jnp.dot(plane, pick, preferred_element_type=F32).astype(BF16)
        put_column(vp_ref, thirds(values), channels, row, -1, pairs)
    plane = 9 * channels
    for i in range(orows):
        for m in (0, pairs - 1, *range(1, pairs - 1)):
            window = vp_ref[m, 2 * i * plane : (2 * i + 3) * plane, :]
            pre = jnp.dot(w_ref[...], window, preferred_element_type=F32)
            sigma = jax.nn.sigmoid(pre)
            hidden = (pre * sigma).astype(BF16)
            h_ref[i, m] = hidden
            if m == 0:
                hl_ref[i] = hidden
            if m == pairs - 1:
                hr_ref[i] = hidden
            slope_ref[i, m] = sigma * (1.0 + pre * (1.0 - sigma))


def shifted(values, steps):
    half = values.shape[1] // 2
    lane = lax.broadcasted_iota(jnp.int32, (values.shape[0], half), 1)
    keep = lane >= steps if steps > 0 else lane < half + steps
    parts = [
        jnp.where(keep, pltpu.roll(values[:, k * half : (k + 1) * half], steps % half, 1), 0.0)
        for k in range(2)
    ]
    return jnp.concatenate(parts, axis=1)


def weights_body(slab_ref, wd_ref, ws_ref, w2_ref, wg_ref, wst_ref):
    outs, width = wd_ref.shape
    mid = width // 27
    wst_ref[...] = ws_ref[...].T

    def fill(src, a):
        for b in range(3):
            block = (a * 3 + b) * 3 * mid
            to = (b * 2 + src) * 3 * mid
            w2_ref[:, to : to + 3 * mid] = wd_ref[:, block : block + 3 * mid]
            for c in range(3):
                tap = wd_ref[:, block + c * mid : block + (c + 1) * mid]
                column = ((2 - b) * 3 + c) * outs
                wg_ref[src * mid : (src + 1) * mid, column : column + outs] = tap.T

    fill(0, 1)

    @pl.when(slab_ref[0] == 0)
    def _():
        fill(1, 2)

    @pl.when(slab_ref[0] != 0)
    def _():
        fill(1, 0)


NT = (((1,), (1,)), ((), ()))


def put_window(ref, at, tile, base, step):
    mid = tile.shape[0]
    wide = tile.astype(F32)
    ref[(*at, slice(base, base + mid))] = shifted(wide, step).astype(BF16)
    ref[(*at, slice(base + mid, base + 2 * mid))] = tile
    ref[(*at, slice(base + 2 * mid, base + 3 * mid))] = shifted(wide, -step).astype(BF16)


def put_residual(out, target, scale, step, pred_ref, rs_ref, at):
    outs = out.shape[0]
    pred_ref[at] = out.astype(BF16)
    res = ((out - target.astype(F32)) * scale).astype(BF16)
    wide = res.astype(F32)
    rs_ref[(*at, slice(0, outs))] = shifted(wide, -step).astype(BF16)
    rs_ref[(*at, slice(outs, 2 * outs))] = res
    rs_ref[(*at, slice(2 * outs, 3 * outs))] = shifted(wide, step).astype(BF16)


def added(parts):
    total = None
    for part in parts:
        total = part if total is None else total + part
    return total


def inner_body(scale, step, h_ref, o_ref, w2_ref, wg_ref, tp_ref, hs_ref, pred_ref, dg_ref, g_ref, rs_ref):
    orows, pairs, mid, lanes = h_ref.shape
    outs = w2_ref.shape[0]
    block = 3 * outs
    for r in range(orows):
        for x in range(pairs):
            put_window(hs_ref, (r, x), h_ref[r, x], 0, step)
            put_window(hs_ref, (r, x), o_ref[r, x], 3 * mid, step)
    for r in range(orows):
        for m in range(1, pairs - 1):
            window = hs_ref[r, m - 1 : m + 2].reshape(18 * mid, lanes)
            out = jnp.dot(w2_ref[...], window, preferred_element_type=F32)
            put_residual(out, tp_ref[r, m], scale, step, pred_ref, rs_ref, (r, m - 1))
    for b in range(3):
        for src in range(2):
            rows = slice(src * 3 * mid, (src + 1) * 3 * mid)
            to = (b * 2 + src) * 3 * mid
            dg_ref[:, to : to + 3 * mid] = added(
                lax.dot_general(
                    rs_ref[r, m - 1, outs : 2 * outs], hs_ref[r, m - 1 + b, rows], NT,
                    preferred_element_type=F32,
                )
                for r in range(orows)
                for m in range(1, pairs - 1)
            )
    for r in range(orows):
        for x in range(1, pairs + 1):
            low, high = max(x - 2, 1), min(x, pairs - 2)
            first = low - (x - 2)
            window = rs_ref[r, low - 1 : high].reshape((high - low + 1) * block, lanes)
            weights = wg_ref[:, first * block : (first + high - low + 1) * block]
            g_ref[r, x - 1] = jnp.dot(weights, window, preferred_element_type=F32)


def outer_body(
    scale, step, hs_ref, hl_ref, hr_ref, ol_ref, or_ref, w2_ref, wg_ref, tp_ref, g_ref,
    pred_ref, res_ref, edge_ref, gown_ref, ghalo_ref, gother_ref, gedge_ref, rs_ref,
):
    orows, pairs, depth, lanes = hs_ref.shape
    mid = depth // 6
    outs = w2_ref.shape[0]
    block = 3 * outs
    ends = (0, pairs - 1)
    for r in range(orows):
        for k, (own, other) in enumerate(((hl_ref, ol_ref), (hr_ref, or_ref))):
            put_window(edge_ref, (r, k), own[r], 0, step)
            put_window(edge_ref, (r, k), other[r], 3 * mid, step)
    for r in range(orows):
        for k, m in enumerate(ends):
            edge = edge_ref[r, k]
            near = hs_ref[r, 0:2] if k == 0 else hs_ref[r, pairs - 2 : pairs]
            near = near.reshape(2 * depth, lanes)
            w_edge = w2_ref[:, :depth] if k == 0 else w2_ref[:, 2 * depth :]
            w_near = w2_ref[:, depth:] if k == 0 else w2_ref[:, : 2 * depth]
            out = jnp.dot(w_edge, edge, preferred_element_type=F32)
            out = out + jnp.dot(w_near, near, preferred_element_type=F32)
            put_residual(out, tp_ref[r, m], scale, step, pred_ref, rs_ref, (r, k))
            res_ref[r, k] = rs_ref[r, k, outs : 2 * outs]
    for r in range(orows):
        for x in range(pairs + 2):
            parts = [g_ref[r, x - 1]] if 0 < x <= pairs else []
            for k, m in enumerate(ends):
                tap = m - (x - 2)
                if 0 <= tap < 3:
                    weights = wg_ref[:, tap * block : (tap + 1) * block]
                    parts.append(jnp.dot(weights, rs_ref[r, k], preferred_element_type=F32))
            grad = added(parts)
            apart = grad[mid:].astype(BF16)
            if 0 < x <= pairs:
                gother_ref[r, x - 1] = apart
            else:
                gedge_ref[x // (pairs + 1), r] = apart
            if x == 0:
                ghalo_ref[0, r] = grad[:mid]
            elif x == pairs + 1:
                ghalo_ref[1, r] = grad[:mid]
            else:
                gown_ref[r, x - 1] = grad[:mid]


def dilated_grad_body(slab_ref, res_ref, hs_ref, edge_ref, dg_ref, mine_ref, send_ref, other_ref):
    orows, pairs, depth, _ = hs_ref.shape
    mid = depth // 6

    def taps(r, m, b):
        x = m - 1 + b
        return edge_ref.at[r, 0] if x < 0 else edge_ref.at[r, 1] if x == pairs else hs_ref.at[r, x]

    for b in range(3):
        columns = slice(b * 3 * mid, (b + 1) * 3 * mid)
        for src in range(2):
            rows = slice(src * 3 * mid, (src + 1) * 3 * mid)
            at = (b * 2 + src) * 3 * mid
            total = dg_ref[:, at : at + 3 * mid] + added(
                lax.dot_general(
                    res_ref[r, k], taps(r, m, b)[rows], NT, preferred_element_type=F32
                )
                for r in range(orows)
                for k, m in enumerate((0, pairs - 1))
            )
            if src == 0:
                split_rows(slab_ref, total, mine_ref, send_ref, columns)
            else:
                strips, count, _ = other_ref.shape
                other_ref[:, :, columns] = total.reshape(strips, count, 3 * mid).astype(BF16)


def split_rows(slab_ref, total, mine_ref, send_ref, columns):
    strips, rows, _ = mine_ref.shape
    parts = total.reshape(strips, 2, rows, total.shape[1])
    first = slab_ref[0] == 0
    mine_ref[:, :, columns] = jnp.where(first, parts[:, 0], parts[:, 1])
    send_ref[:, :, columns] = jnp.where(first, parts[:, 1], parts[:, 0]).astype(BF16)


def strided_part(gown_ref, gx_ref, extra, slope_ref, vp_ref, columns):
    orows = gown_ref.shape[0]
    plane = vp_ref.shape[1] // (2 * orows + 1)

    def part(i, m):
        grad = gown_ref[i, m] + gx_ref[i, m].astype(F32)
        if m in extra:
            grad = grad + extra[m][i].astype(F32)
        pg = (grad * slope_ref[i, m]).astype(BF16)
        window = vp_ref[m, 2 * i * plane : (2 * i + 3) * plane, :]
        return lax.dot_general(pg, window, NT, preferred_element_type=F32)

    return added(part(i, m) for i in range(orows) for m in columns)


def strided_inner_body(gown_ref, gx_ref, slope_ref, vp_ref, sum_ref):
    pairs = gown_ref.shape[1]
    sum_ref[...] = strided_part(gown_ref, gx_ref, {}, slope_ref, vp_ref, range(1, pairs - 1))


def strided_grad_body(
    slab_ref, gown_ref, gx_ref, gl_ref, gr_ref, slope_ref, vp_ref, sum_ref, mine_ref, send_ref
):
    pairs, mid = gown_ref.shape[1:3]
    extra = {0: gl_ref, pairs - 1: gr_ref}
    total = sum_ref[...] + strided_part(
        gown_ref, gx_ref, extra, slope_ref, vp_ref, (0, pairs - 1)
    )
    width = mine_ref.shape[2]
    pad = jnp.zeros((mid, 2 * width - total.shape[1]), F32)
    low, high = total[:, :width], jnp.concatenate([total[:, width:], pad], axis=1)
    first = slab_ref[0] == 0
    mine_ref[...] = jnp.where(first, low, high).reshape(mine_ref.shape)
    send_ref[...] = jnp.where(first, high, low).reshape(mine_ref.shape).astype(BF16)


def prediction_body(inner_ref, outer_ref, out_ref, tall_ref):
    orows, inner, outs, lanes = inner_ref.shape
    half = lanes // 2
    cols = 2 * (inner + 2)
    for r in range(orows):
        slot = r % 2
        for col in range(cols):
            m = col // 2
            tile = outer_ref.at[r, m // (inner + 1)] if m in (0, inner + 1) else inner_ref.at[r, m - 1]
            values = tile[:, (col % 2) * half : (col % 2 + 1) * half]
            tall_ref[slot, pl.ds(col, outs, stride=cols), :] = values.astype(F32)
        out_ref[:, r] = tall_ref[slot].reshape(outs, cols, half).astype(BF16)


def sds(shape, dtype):
    return jax.ShapeDtypeStruct(shape, dtype)


def shift_along(value, axis, steps):
    count = lax.axis_size(axis)
    pairs = [(i, i + steps) for i in range(count) if 0 <= i + steps < count]
    return lax.ppermute(value, axis, pairs)


def swap(value):
    return lax.ppermute(value, "slab", [(0, 1), (1, 0)])


def local(volume, target, strided_weight, dilated_weight):
    channels, rows_in, cols_in, depth = volume.shape
    mid = strided_weight.shape[0]
    outs = dilated_weight.shape[0]
    orows, ocols, half = rows_in // 2, cols_in // 2, depth // 2
    pairs, lanes = ocols // 2, 2 * half
    strips = lax.axis_size("strip")
    slab = lax.axis_index("slab")
    strip = lax.axis_index("strip")
    groups = strips // 2
    place, parity = strip // 2, strip % 2
    scalars = (slab == 0, slab, parity, 1 - parity, *((place + d) % groups for d in range(groups)))
    edge = vmem_call(
        edge_body,
        sds((rows_in, channels, depth), BF16),
        0,
        [VMEM((channels, rows_in, min(8, cols_in), depth), BF16), pltpu.SemaphoreType.DMA(())],
        in_hbm=1,
    )(volume)
    edge, scalars = lax.optimization_barrier((edge, scalars))
    first, slab, parity, other_parity, *places = scalars
    slab_id = slab.reshape(1).astype(jnp.int32)
    step = 2
    assert lax.axis_size("slab") == 2 and orows == step and ocols % 2 == 0
    cells = orows * ocols * half * lax.axis_size("slab") * strips
    scale = 1.0 / math.sqrt(cells)

    left = shift_along(edge, "strip", 1)
    vp, plane = vmem_call(
        split_body,
        (
            sds((pairs, (rows_in + 1) * 9 * channels, lanes), BF16),
            sds((channels * cols_in, depth), BF16),
        ),
        1,
        [VMEM((2, 3, channels * cols_in, half), F32)],
    )(volume)
    left, vp, plane = lax.optimization_barrier((left, vp, plane))
    lower = shift_along(jnp.concatenate([plane, left[-1]], axis=0), "slab", 1)

    w2, wg, ws = vmem_call(
        weights_body,
        (
            sds((outs, 18 * mid), BF16),
            sds((2 * mid, 9 * outs), BF16),
            sds((mid, 27 * channels), BF16),
        ),
        2,
        scalars=1,
    )(slab_id, dilated_weight, strided_weight.T)
    tp = vmem_call(
        target_body,
        sds((orows, pairs, outs, lanes), BF16),
        1,
        [VMEM((2, outs * ocols, half), F32)],
    )(target)
    vp, hidden, hid_l, hid_r, slope = vmem_call(
        preact_body,
        (
            sds(vp.shape, BF16),
            sds((orows, pairs, mid, lanes), BF16),
            sds((orows, mid, lanes), BF16),
            sds((orows, mid, lanes), BF16),
            sds((orows, pairs, mid, lanes), F32),
        ),
        4,
        [VMEM((3, channels * cols_in, half), F32)],
    )(vp, lower, left, ws)

    from_left = shift_along(hid_r, "strip", 1)
    from_right = shift_along(hid_l, "strip", -1)
    other = swap(hidden)

    def inner(*refs):
        inner_body(scale, step, *refs)

    def outer(*refs):
        outer_body(scale, step, *refs)

    hs, pred_in, dg_in, g_in = vmem_call(
        inner,
        (
            sds((orows, pairs, 6 * mid, lanes), BF16),
            sds((orows, pairs - 2, outs, lanes), BF16),
            sds((outs, 18 * mid), F32),
            sds((orows, pairs, 2 * mid, lanes), F32),
        ),
        5,
        [VMEM((orows, pairs - 2, 3 * outs, lanes), BF16)],
    )(hidden, other, w2, wg, tp)

    from_left, from_right, hs = lax.optimization_barrier((from_left, from_right, hs))
    other_left = swap(from_left)
    other_right = swap(from_right)

    pred_out, residual, edges, gown, ghalo, gother, gedge = vmem_call(
        outer,
        (
            sds((orows, 2, outs, lanes), BF16),
            sds((orows, 2, outs, lanes), BF16),
            sds((orows, 2, 6 * mid, lanes), BF16),
            sds((orows, pairs, mid, lanes), F32),
            sds((2, orows, mid, lanes), F32),
            sds((orows, pairs, mid, lanes), BF16),
            sds((2, orows, mid, lanes), BF16),
        ),
        9,
        [VMEM((orows, 2, 3 * outs, lanes), BF16)],
    )(hs, from_left, from_right, other_left, other_right, w2, wg, tp, g_in)

    gx_edge = swap(gedge)
    gx = swap(gother)
    to_left = (ghalo[0] + gx_edge[0].astype(F32)).astype(BF16)
    to_right = (ghalo[1] + gx_edge[1].astype(F32)).astype(BF16)
    grad_l = shift_along(to_right, "strip", 1)
    grad_r = shift_along(to_left, "strip", -1)

    rows = outs // strips
    half_rows = rows // 2
    mine, send, apart = vmem_call(
        dilated_grad_body,
        (
            sds((strips, half_rows, 9 * mid), F32),
            sds((strips, half_rows, 9 * mid), BF16),
            sds((strips, rows, 9 * mid), BF16),
        ),
        4,
        scalars=1,
    )(slab_id, residual, hs, edges, dg_in)

    def pick(array, index, dim):
        return lax.dynamic_index_in_dim(array, index, dim, False, allow_negative_indices=False)

    def pair_swap(value):
        return lax.ppermute(value, "strip", [(i, i ^ 1) for i in range(strips)])

    def far_swap(chunks):
        return [
            lax.ppermute(
                pick(chunks, places[d], 0).astype(BF16),
                "strip",
                [(i, (i + 2 * d) % strips) for i in range(strips)],
            )
            for d in range(1, groups)
        ]

    def far_sum(chunks, got):
        return added([pick(chunks, places[0], 0).astype(F32), *(g.astype(F32) for g in got)])

    apart = apart.reshape(groups, 2, rows, 9 * mid)
    apart_got = pair_swap(pick(apart, other_parity, 1))
    dg_own = (mine + swap(send).astype(F32)).astype(BF16)

    prediction = vmem_call(
        prediction_body,
        sds((outs, orows, ocols, half), BF16),
        2,
        [VMEM((2, outs * ocols, half), F32)],
    )(pred_in, pred_out)
    sg_in = vmem_call(strided_inner_body, sds((mid, 27 * channels), F32), 4)(gown, gx, slope, vp)
    mid_rows = mid // strips
    width = 9 * mid
    assert width < 27 * channels <= 2 * width
    dg_own, prediction = lax.optimization_barrier((dg_own, prediction))
    dg_own = dg_own.reshape(groups, 2, half_rows, 9 * mid)
    own_got = far_swap(dg_own)
    grad_l, grad_r, apart_got, sg_in = lax.optimization_barrier((grad_l, grad_r, apart_got, sg_in))
    smine, ssend = vmem_call(
        strided_grad_body,
        (sds((strips, mid_rows, width), F32), sds((strips, mid_rows, width), BF16)),
        7,
        scalars=1,
    )(slab_id, gown, gx, grad_l, grad_r, slope, vp, sg_in)
    sg = (smine + swap(ssend).astype(F32)).astype(BF16).reshape(groups, 2, mid_rows, width)
    own = far_sum(dg_own, own_got)
    sent = jnp.concatenate(
        [
            pick(sg, other_parity, 1).reshape(groups * mid_rows, width),
            pick(own, other_parity, 0).astype(BF16),
        ],
        axis=0,
    )
    got = pair_swap(sent).astype(F32)
    own = pick(own, parity, 0) + got[groups * mid_rows :]
    sg = pick(sg, parity, 1).astype(F32) + got[: groups * mid_rows].reshape(groups, mid_rows, width)
    dg = pick(apart, parity, 1).astype(F32) + apart_got.astype(F32)
    total = jnp.concatenate([dg, sg], axis=1)
    total = jnp.concatenate([own, far_sum(total, far_swap(total))], axis=0)
    across = swap(total)
    low, high = jnp.where(first, total, across), jnp.where(first, across, total)
    middle = jnp.concatenate([low[:half_rows], high[:half_rows]], axis=0)
    end = half_rows + rows
    dilated_grad = jnp.concatenate([high[half_rows:end], middle, low[half_rows:end]], axis=1)
    strided_grad = jnp.concatenate([low[end:], high[end:, : 27 * channels - width]], axis=1)
    return prediction, strided_grad, dilated_grad


def solution(mesh):
    return jax.shard_map(
        local,
        mesh=mesh,
        in_specs=(P("fold", "slab", "strip", None), P("fold", "slab", "strip", None), P(), P()),
        out_specs=(
            P("fold", "slab", "strip", None),
            P(("fold", "strip"), None),
            P(("fold", "strip"), None),
        ),
        check_vma=False,
    )
```

```python
import math

import jax
import jax.numpy as jnp
from jax import lax
from jax.experimental import pallas as pl
from jax.experimental.pallas import tpu as pltpu
from jax.sharding import PartitionSpec as P


BF16 = jnp.bfloat16
F32 = jnp.float32
VMEM = pltpu.VMEM
VMEM_LIMIT = 20 * 1024 * 1024


def vmem_call(body, out_shape, n_in, scratch=(), scalars=0, in_hbm=0):
    spec = pl.BlockSpec(memory_space=pltpu.VMEM)
    scalar = pl.BlockSpec(memory_space=pltpu.SMEM)
    hbm = pl.BlockSpec(memory_space=pltpu.HBM)
    return pl.pallas_call(
        body,
        out_shape=out_shape,
        in_specs=[scalar] * scalars + [hbm] * in_hbm + [spec] * n_in,
        out_specs=jax.tree.map(lambda _: spec, out_shape),
        scratch_shapes=list(scratch),
        compiler_params=pltpu.CompilerParams(vmem_limit_bytes=VMEM_LIMIT),
    )


def selection(depth):
    half = depth // 2
    source = lax.broadcasted_iota(jnp.int32, (depth, 3 * half), 0)
    lane = lax.broadcasted_iota(jnp.int32, (depth, 3 * half), 1)
    even = (lane < half) & (source == 2 * lane)
    odd = (lane >= half) & (lane < 2 * half) & (source == 2 * (lane - half) + 1)
    late = (lane >= 2 * half) & (source == 2 * (lane - 2 * half) - 1)
    return jnp.where(even | odd | late, 1.0, 0.0).astype(BF16)


def thirds(values):
    half = values.shape[1] // 3
    return [values[:, k * half : (k + 1) * half] for k in range(3)]


def spread(plane, pick, scratch):
    for k, part in enumerate(thirds(jnp.dot(plane, pick, preferred_element_type=F32))):
        scratch[k] = part


def put_column(vp_ref, values, channels, row, col, pairs):
    half = values[0].shape[1]
    taps = (values[2], values[0], values[1])
    for b in range(3):
        for h in range(2):
            rest = col + 1 - b - 2 * h
            if rest % 4 or not 0 <= rest // 4 < pairs:
                continue
            for c in range(3):
                start = ((row * 3 + b) * 3 + c) * channels
                vp_ref[rest // 4, start : start + channels, h * half : (h + 1) * half] = taps[c]


def edge_body(vol_ref, edge_ref, half_ref, sem):
    channels, rows, cols, depth = vol_ref.shape
    count = half_ref.shape[2]
    copy = pltpu.make_async_copy(vol_ref.at[:, :, cols - count :], half_ref, sem)
    copy.start()
    channel = lax.broadcasted_iota(jnp.int32, (channels, channels * count), 0)
    source = lax.broadcasted_iota(jnp.int32, (channels, channels * count), 1)
    last = jnp.where(source == channel * count + count - 1, 1.0, 0.0).astype(BF16)
    copy.wait()
    for row in range(rows):
        plane = half_ref[:, row].astype(F32).reshape(channels * count, depth).astype(BF16)
        edge_ref[row] = jnp.dot(last, plane, preferred_element_type=F32).astype(BF16)


def split_body(vol_ref, vp_ref, last_ref, wide_ref):
    channels, rows, cols, depth = vol_ref.shape
    pairs = cols // 4
    pick = selection(depth)
    for row in range(rows):
        slot = row % 2
        plane = vol_ref[:, row].reshape(channels * cols, depth)
        if row == rows - 1:
            last_ref[...] = plane
        spread(plane, pick, wide_ref.at[slot])
        for col in range(cols):
            values = [
                wide_ref[slot, k, pl.ds(col, channels, stride=cols), :].astype(BF16)
                for k in range(3)
            ]
            put_column(vp_ref, values, channels, row + 1, col, pairs)


def target_body(tgt_ref, tp_ref, tall_ref):
    outs, orows, ocols, half = tgt_ref.shape
    for row in range(orows):
        slot = row % 2
        tall_ref[slot] = tgt_ref[:, row].astype(F32).reshape(outs * ocols, half)
        for col in range(ocols):
            values = tall_ref[slot, pl.ds(col, outs, stride=ocols), :].astype(BF16)
            tp_ref[row, col // 2, :, (col % 2) * half : (col % 2 + 1) * half] = values


def preact_body(own_ref, hrow_ref, hcol_ref, w_ref, vp_ref, h_ref, hl_ref, hr_ref, slope_ref, wide_ref):
    rows_in, channels, depth = hcol_ref.shape
    size = hrow_ref.shape[0] - channels
    cols = size // channels
    orows, pairs, _, _ = h_ref.shape
    vp_ref[:, 9 * channels :] = own_ref[:, 9 * channels :]
    pick = selection(depth)
    spread(hrow_ref[:size], pick, wide_ref)
    for col in range(cols):
        values = [
            wide_ref[k, pl.ds(col, channels, stride=cols), :].astype(BF16) for k in range(3)
        ]
        put_column(vp_ref, values, channels, 0, col, pairs)
    for row in range(rows_in + 1):
        plane = hrow_ref[size:] if row == 0 else hcol_ref[row - 1]
        values = jnp.dot(plane, pick, preferred_element_type=F32).astype(BF16)
        put_column(vp_ref, thirds(values), channels, row, -1, pairs)
    plane = 9 * channels
    for i in range(orows):
        for m in (0, pairs - 1, *range(1, pairs - 1)):
            window = vp_ref[m, 2 * i * plane : (2 * i + 3) * plane, :]
            pre = jnp.dot(w_ref[...], window, preferred_element_type=F32)
            sigma = jax.nn.sigmoid(pre)
            hidden = (pre * sigma).astype(BF16)
            h_ref[i, m] = hidden
            if m == 0:
                hl_ref[i] = hidden
            if m == pairs - 1:
                hr_ref[i] = hidden
            slope_ref[i, m] = sigma * (1.0 + pre * (1.0 - sigma))


def shifted(values, steps):
    half = values.shape[1] // 2
    lane = lax.broadcasted_iota(jnp.int32, (values.shape[0], half), 1)
    keep = lane >= steps if steps > 0 else lane < half + steps
    parts = [
        jnp.where(keep, pltpu.roll(values[:, k * half : (k + 1) * half], steps % half, 1), 0.0)
        for k in range(2)
    ]
    return jnp.concatenate(parts, axis=1)


def weights_body(slab_ref, wd_ref, ws_ref, w2_ref, wg_ref, wst_ref):
    outs, width = wd_ref.shape
    mid = width // 27
    wst_ref[...] = ws_ref[...].T

    def fill(src, a):
        for b in range(3):
            block = (a * 3 + b) * 3 * mid
            to = (b * 2 + src) * 3 * mid
            w2_ref[:, to : to + 3 * mid] = wd_ref[:, block : block + 3 * mid]
            for c in range(3):
                tap = wd_ref[:, block + c * mid : block + (c + 1) * mid]
                column = ((2 - b) * 3 + c) * outs
                wg_ref[src * mid : (src + 1) * mid, column : column + outs] = tap.T

    fill(0, 1)

    @pl.when(slab_ref[0] == 0)
    def _():
        fill(1, 2)

    @pl.when(slab_ref[0] != 0)
    def _():
        fill(1, 0)


NT = (((1,), (1,)), ((), ()))


def put_window(ref, at, tile, base, step):
    mid = tile.shape[0]
    wide = tile.astype(F32)
    ref[(*at, slice(base, base + mid))] = shifted(wide, step).astype(BF16)
    ref[(*at, slice(base + mid, base + 2 * mid))] = tile
    ref[(*at, slice(base + 2 * mid, base + 3 * mid))] = shifted(wide, -step).astype(BF16)


def put_residual(out, target, scale, step, pred_ref, rs_ref, at):
    outs = out.shape[0]
    pred_ref[at] = out.astype(BF16)
    res = ((out - target.astype(F32)) * scale).astype(BF16)
    wide = res.astype(F32)
    rs_ref[(*at, slice(0, outs))] = shifted(wide, -step).astype(BF16)
    rs_ref[(*at, slice(outs, 2 * outs))] = res
    rs_ref[(*at, slice(2 * outs, 3 * outs))] = shifted(wide, step).astype(BF16)


def added(parts):
    total = None
    for part in parts:
        total = part if total is None else total + part
    return total


def inner_body(scale, step, h_ref, o_ref, w2_ref, wg_ref, tp_ref, hs_ref, pred_ref, dg_ref, g_ref, rs_ref):
    orows, pairs, mid, lanes = h_ref.shape
    outs = w2_ref.shape[0]
    block = 3 * outs
    for r in range(orows):
        for x in range(pairs):
            put_window(hs_ref, (r, x), h_ref[r, x], 0, step)
            put_window(hs_ref, (r, x), o_ref[r, x], 3 * mid, step)
    for r in range(orows):
        for m in range(1, pairs - 1):
            window = hs_ref[r, m - 1 : m + 2].reshape(18 * mid, lanes)
            out = jnp.dot(w2_ref[...], window, preferred_element_type=F32)
            put_residual(out, tp_ref[r, m], scale, step, pred_ref, rs_ref, (r, m - 1))
    for b in range(3):
        for src in range(2):
            rows = slice(src * 3 * mid, (src + 1) * 3 * mid)
            to = (b * 2 + src) * 3 * mid
            dg_ref[:, to : to + 3 * mid] = added(
                lax.dot_general(
                    rs_ref[r, m - 1, outs : 2 * outs], hs_ref[r, m - 1 + b, rows], NT,
                    preferred_element_type=F32,
                )
                for r in range(orows)
                for m in range(1, pairs - 1)
            )
    for r in range(orows):
        for x in range(1, pairs + 1):
            low, high = max(x - 2, 1), min(x, pairs - 2)
            first = low - (x - 2)
            window = rs_ref[r, low - 1 : high].reshape((high - low + 1) * block, lanes)
            weights = wg_ref[:, first * block : (first + high - low + 1) * block]
            g_ref[r, x - 1] = jnp.dot(weights, window, preferred_element_type=F32)


def outer_body(
    scale, step, hs_ref, hl_ref, hr_ref, ol_ref, or_ref, w2_ref, wg_ref, tp_ref, g_ref,
    pred_ref, res_ref, edge_ref, gown_ref, ghalo_ref, gother_ref, gedge_ref, rs_ref,
):
    orows, pairs, depth, lanes = hs_ref.shape
    mid = depth // 6
    outs = w2_ref.shape[0]
    block = 3 * outs
    ends = (0, pairs - 1)
    for r in range(orows):
        for k, (own, other) in enumerate(((hl_ref, ol_ref), (hr_ref, or_ref))):
            put_window(edge_ref, (r, k), own[r], 0, step)
            put_window(edge_ref, (r, k), other[r], 3 * mid, step)
    for r in range(orows):
        for k, m in enumerate(ends):
            edge = edge_ref[r, k]
            near = hs_ref[r, 0:2] if k == 0 else hs_ref[r, pairs - 2 : pairs]
            near = near.reshape(2 * depth, lanes)
            w_edge = w2_ref[:, :depth] if k == 0 else w2_ref[:, 2 * depth :]
            w_near = w2_ref[:, depth:] if k == 0 else w2_ref[:, : 2 * depth]
            out = jnp.dot(w_edge, edge, preferred_element_type=F32)
            out = out + jnp.dot(w_near, near, preferred_element_type=F32)
            put_residual(out, tp_ref[r, m], scale, step, pred_ref, rs_ref, (r, k))
            res_ref[r, k] = rs_ref[r, k, outs : 2 * outs]
    for r in range(orows):
        for x in range(pairs + 2):
            parts = [g_ref[r, x - 1]] if 0 < x <= pairs else []
            for k, m in enumerate(ends):
                tap = m - (x - 2)
                if 0 <= tap < 3:
                    weights = wg_ref[:, tap * block : (tap + 1) * block]
                    parts.append(jnp.dot(weights, rs_ref[r, k], preferred_element_type=F32))
            grad = added(parts)
            apart = grad[mid:].astype(BF16)
            if 0 < x <= pairs:
                gother_ref[r, x - 1] = apart
            else:
                gedge_ref[x // (pairs + 1), r] = apart
            if x == 0:
                ghalo_ref[0, r] = grad[:mid]
            elif x == pairs + 1:
                ghalo_ref[1, r] = grad[:mid]
            else:
                gown_ref[r, x - 1] = grad[:mid]


def dilated_grad_body(slab_ref, res_ref, hs_ref, edge_ref, dg_ref, mine_ref, send_ref, other_ref):
    orows, pairs, depth, _ = hs_ref.shape
    mid = depth // 6

    def taps(r, m, b):
        x = m - 1 + b
        return edge_ref.at[r, 0] if x < 0 else edge_ref.at[r, 1] if x == pairs else hs_ref.at[r, x]

    for b in range(3):
        columns = slice(b * 3 * mid, (b + 1) * 3 * mid)
        for src in range(2):
            rows = slice(src * 3 * mid, (src + 1) * 3 * mid)
            at = (b * 2 + src) * 3 * mid
            total = dg_ref[:, at : at + 3 * mid] + added(
                lax.dot_general(
                    res_ref[r, k], taps(r, m, b)[rows], NT, preferred_element_type=F32
                )
                for r in range(orows)
                for k, m in enumerate((0, pairs - 1))
            )
            if src == 0:
                split_rows(slab_ref, total, mine_ref, send_ref, columns)
            else:
                strips, count, _ = other_ref.shape
                other_ref[:, :, columns] = total.reshape(strips, count, 3 * mid).astype(BF16)


def split_rows(slab_ref, total, mine_ref, send_ref, columns):
    strips, rows, _ = mine_ref.shape
    parts = total.reshape(strips, 2, rows, total.shape[1])
    first = slab_ref[0] == 0
    mine_ref[:, :, columns] = jnp.where(first, parts[:, 0], parts[:, 1])
    send_ref[:, :, columns] = jnp.where(first, parts[:, 1], parts[:, 0]).astype(BF16)


def strided_part(gown_ref, gx_ref, extra, slope_ref, vp_ref, columns):
    orows = gown_ref.shape[0]
    plane = vp_ref.shape[1] // (2 * orows + 1)

    def part(i, m):
        grad = gown_ref[i, m] + gx_ref[i, m].astype(F32)
        if m in extra:
            grad = grad + extra[m][i].astype(F32)
        pg = (grad * slope_ref[i, m]).astype(BF16)
        window = vp_ref[m, 2 * i * plane : (2 * i + 3) * plane, :]
        return lax.dot_general(pg, window, NT, preferred_element_type=F32)

    return added(part(i, m) for i in range(orows) for m in columns)


def strided_inner_body(gown_ref, gx_ref, slope_ref, vp_ref, sum_ref):
    pairs = gown_ref.shape[1]
    sum_ref[...] = strided_part(gown_ref, gx_ref, {}, slope_ref, vp_ref, range(1, pairs - 1))


def strided_grad_body(
    slab_ref, gown_ref, gx_ref, gl_ref, gr_ref, slope_ref, vp_ref, sum_ref, mine_ref, send_ref
):
    pairs, mid = gown_ref.shape[1:3]
    extra = {0: gl_ref, pairs - 1: gr_ref}
    total = sum_ref[...] + strided_part(
        gown_ref, gx_ref, extra, slope_ref, vp_ref, (0, pairs - 1)
    )
    width = mine_ref.shape[2]
    pad = jnp.zeros((mid, 2 * width - total.shape[1]), F32)
    low, high = total[:, :width], jnp.concatenate([total[:, width:], pad], axis=1)
    first = slab_ref[0] == 0
    mine_ref[...] = jnp.where(first, low, high).reshape(mine_ref.shape)
    send_ref[...] = jnp.where(first, high, low).reshape(mine_ref.shape).astype(BF16)


def prediction_body(inner_ref, outer_ref, out_ref, tall_ref):
    orows, inner, outs, lanes = inner_ref.shape
    half = lanes // 2
    cols = 2 * (inner + 2)
    for r in range(orows):
        slot = r % 2
        for col in range(cols):
            m = col // 2
            tile = outer_ref.at[r, m // (inner + 1)] if m in (0, inner + 1) else inner_ref.at[r, m - 1]
            values = tile[:, (col % 2) * half : (col % 2 + 1) * half]
            tall_ref[slot, pl.ds(col, outs, stride=cols), :] = values.astype(F32)
        out_ref[:, r] = tall_ref[slot].reshape(outs, cols, half).astype(BF16)


def sds(shape, dtype):
    return jax.ShapeDtypeStruct(shape, dtype)


def shift_along(value, axis, steps):
    count = lax.axis_size(axis)
    pairs = [(i, i + steps) for i in range(count) if 0 <= i + steps < count]
    return lax.ppermute(value, axis, pairs)


def swap(value):
    return lax.ppermute(value, "slab", [(0, 1), (1, 0)])


def local(volume, target, strided_weight, dilated_weight):
    channels, rows_in, cols_in, depth = volume.shape
    mid = strided_weight.shape[0]
    outs = dilated_weight.shape[0]
    orows, ocols, half = rows_in // 2, cols_in // 2, depth // 2
    pairs, lanes = ocols // 2, 2 * half
    strips = lax.axis_size("strip")
    slab = lax.axis_index("slab")
    strip = lax.axis_index("strip")
    groups = strips // 2
    place, parity = strip // 2, strip % 2
    scalars = (slab == 0, slab, parity, 1 - parity, *((place + d) % groups for d in range(groups)))
    edge = vmem_call(
        edge_body,
        sds((rows_in, channels, depth), BF16),
        0,
        [VMEM((channels, rows_in, min(8, cols_in), depth), BF16), pltpu.SemaphoreType.DMA(())],
        in_hbm=1,
    )(volume)
    edge, scalars = lax.optimization_barrier((edge, scalars))
    first, slab, parity, other_parity, *places = scalars
    slab_id = slab.reshape(1).astype(jnp.int32)
    step = 2
    assert lax.axis_size("slab") == 2 and orows == step and ocols % 2 == 0
    cells = orows * ocols * half * lax.axis_size("slab") * strips
    scale = 1.0 / math.sqrt(cells)

    left = shift_along(edge, "strip", 1)
    vp, plane = vmem_call(
        split_body,
        (
            sds((pairs, (rows_in + 1) * 9 * channels, lanes), BF16),
            sds((channels * cols_in, depth), BF16),
        ),
        1,
        [VMEM((2, 3, channels * cols_in, half), F32)],
    )(volume)
    left, vp, plane = lax.optimization_barrier((left, vp, plane))
    lower = shift_along(jnp.concatenate([plane, left[-1]], axis=0), "slab", 1)

    w2, wg, ws = vmem_call(
        weights_body,
        (
            sds((outs, 18 * mid), BF16),
            sds((2 * mid, 9 * outs), BF16),
            sds((mid, 27 * channels), BF16),
        ),
        2,
        scalars=1,
    )(slab_id, dilated_weight, strided_weight.T)
    tp = vmem_call(
        target_body,
        sds((orows, pairs, outs, lanes), BF16),
        1,
        [VMEM((2, outs * ocols, half), F32)],
    )(target)
    vp, hidden, hid_l, hid_r, slope = vmem_call(
        preact_body,
        (
            sds(vp.shape, BF16),
            sds((orows, pairs, mid, lanes), BF16),
            sds((orows, mid, lanes), BF16),
            sds((orows, mid, lanes), BF16),
            sds((orows, pairs, mid, lanes), F32),
        ),
        4,
        [VMEM((3, channels * cols_in, half), F32)],
    )(vp, lower, left, ws)

    from_left = shift_along(hid_r, "strip", 1)
    from_right = shift_along(hid_l, "strip", -1)
    other = swap(hidden)

    def inner(*refs):
        inner_body(scale, step, *refs)

    def outer(*refs):
        outer_body(scale, step, *refs)

    hs, pred_in, dg_in, g_in = vmem_call(
        inner,
        (
            sds((orows, pairs, 6 * mid, lanes), BF16),
            sds((orows, pairs - 2, outs, lanes), BF16),
            sds((outs, 18 * mid), F32),
            sds((orows, pairs, 2 * mid, lanes), F32),
        ),
        5,
        [VMEM((orows, pairs - 2, 3 * outs, lanes), BF16)],
    )(hidden, other, w2, wg, tp)

    from_left, from_right, hs = lax.optimization_barrier((from_left, from_right, hs))
    other_left = swap(from_left)
    other_right = swap(from_right)

    pred_out, residual, edges, gown, ghalo, gother, gedge = vmem_call(
        outer,
        (
            sds((orows, 2, outs, lanes), BF16),
            sds((orows, 2, outs, lanes), BF16),
            sds((orows, 2, 6 * mid, lanes), BF16),
            sds((orows, pairs, mid, lanes), F32),
            sds((2, orows, mid, lanes), F32),
            sds((orows, pairs, mid, lanes), BF16),
            sds((2, orows, mid, lanes), BF16),
        ),
        9,
        [VMEM((orows, 2, 3 * outs, lanes), BF16)],
    )(hs, from_left, from_right, other_left, other_right, w2, wg, tp, g_in)

    gx_edge = swap(gedge)
    gx = swap(gother)
    to_left = (ghalo[0] + gx_edge[0].astype(F32)).astype(BF16)
    to_right = (ghalo[1] + gx_edge[1].astype(F32)).astype(BF16)
    grad_l = shift_along(to_right, "strip", 1)
    grad_r = shift_along(to_left, "strip", -1)

    rows = outs // strips
    half_rows = rows // 2
    mine, send, apart = vmem_call(
        dilated_grad_body,
        (
            sds((strips, half_rows, 9 * mid), F32),
            sds((strips, half_rows, 9 * mid), BF16),
            sds((strips, rows, 9 * mid), BF16),
        ),
        4,
        scalars=1,
    )(slab_id, residual, hs, edges, dg_in)

    def pick(array, index, dim):
        return lax.dynamic_index_in_dim(array, index, dim, False, allow_negative_indices=False)

    def pair_swap(value):
        return lax.ppermute(value, "strip", [(i, i ^ 1) for i in range(strips)])

    def far_swap(chunks):
        return [
            lax.ppermute(
                pick(chunks, places[d], 0).astype(BF16),
                "strip",
                [(i, (i + 2 * d) % strips) for i in range(strips)],
            )
            for d in range(1, groups)
        ]

    def far_sum(chunks, got):
        return added([pick(chunks, places[0], 0).astype(F32), *(g.astype(F32) for g in got)])

    apart = apart.reshape(groups, 2, rows, 9 * mid)
    apart_got = pair_swap(pick(apart, other_parity, 1))
    dg_own = (mine + swap(send).astype(F32)).astype(BF16)

    mid_rows = mid // strips
    width = 9 * mid
    assert width < 27 * channels <= 2 * width
    dg_own, gx = lax.optimization_barrier((dg_own, gx))
    dg_own = dg_own.reshape(groups, 2, half_rows, 9 * mid)
    own_got = far_swap(dg_own)
    sg_in = vmem_call(strided_inner_body, sds((mid, 27 * channels), F32), 4)(gown, gx, slope, vp)
    grad_l, grad_r, sg_in = lax.optimization_barrier((grad_l, grad_r, sg_in))
    smine, ssend = vmem_call(
        strided_grad_body,
        (sds((strips, mid_rows, width), F32), sds((strips, mid_rows, width), BF16)),
        7,
        scalars=1,
    )(slab_id, gown, gx, grad_l, grad_r, slope, vp, sg_in)
    pred_out, ssend = lax.optimization_barrier((pred_out, ssend))
    prediction = vmem_call(
        prediction_body,
        sds((outs, orows, ocols, half), BF16),
        2,
        [VMEM((2, outs * ocols, half), F32)],
    )(pred_in, pred_out)
    sg = (smine + swap(ssend).astype(F32)).astype(BF16).reshape(groups, 2, mid_rows, width)
    own = far_sum(dg_own, own_got)
    sent = jnp.concatenate(
        [
            pick(sg, other_parity, 1).reshape(groups * mid_rows, width),
            pick(own, other_parity, 0).astype(BF16),
        ],
        axis=0,
    )
    sent, apart_got = lax.optimization_barrier((sent, apart_got))
    got = pair_swap(sent).astype(F32)
    own = pick(own, parity, 0) + got[groups * mid_rows :]
    sg = pick(sg, parity, 1).astype(F32) + got[: groups * mid_rows].reshape(groups, mid_rows, width)
    dg = pick(apart, parity, 1).astype(F32) + apart_got.astype(F32)
    total = jnp.concatenate([dg, sg], axis=1)
    total = jnp.concatenate([own, far_sum(total, far_swap(total))], axis=0)
    across = swap(total)
    low, high = jnp.where(first, total, across), jnp.where(first, across, total)
    middle = jnp.concatenate([low[:half_rows], high[:half_rows]], axis=0)
    end = half_rows + rows
    dilated_grad = jnp.concatenate([high[half_rows:end], middle, low[half_rows:end]], axis=1)
    strided_grad = jnp.concatenate([low[end:], high[end:, : 27 * channels - width]], axis=1)
    return prediction, strided_grad, dilated_grad


def solution(mesh):
    return jax.shard_map(
        local,
        mesh=mesh,
        in_specs=(P("fold", "slab", "strip", None), P("fold", "slab", "strip", None), P(), P()),
        out_specs=(
            P("fold", "slab", "strip", None),
            P(("fold", "strip"), None),
            P(("fold", "strip"), None),
        ),
        check_vma=False,
    )
```
